32 devices in a mesh: tm: 8 (over y, x, core), sector: 4 (over z).
Axes of the slice: x: 2, y: 2, z: 4, core: 2. Of those that a mesh axis runs over, the one named last changes fastest.
Arguments:
- propagator: bfloat16 [4, 8, 640, 640], P('sector', 'tm'), may hold values from -6 to 6
- rising_op: bfloat16 [4, 640, 640], P('sector'), may hold values from -0.25 to 0.25
- energies: float32 [4, 640], P('sector'), may hold values from 0.5 to 40
- hyb_particle: float32 [8], P('tm'), may hold values from 0.2 to 1
- hyb_hole: float32 [8], P('tm'), may hold values from 0.2 to 1
- sector_sizes: int32 [4], P('sector'), may hold values from 160 to 640, as said below
Outputs:
- new_prop: bfloat16 [4, 8, 640, 640], P('sector', 'tm')
The draws below stay inside these ranges and needn't reach their ends.
Inputs may be any that keep to these rules, and one draw needn't show every extreme that they name: `sector_sizes`: one sector holds exactly 640 states.
All inputs are finite; a program needn't handle non-finite values.
Results may differ from the reference program's by a relative error of at most 0.0061.
Values may be sent and summed in bfloat16 or wider, within the bound.
A program may use at most 128 MiB of HBM per device.

```python
import math
import jax
import jax.numpy as jnp
from jax import lax

B = 640
SECT = 4
TIMES = 8


def draw_sector_sizes(key, part):
    first_key = jax.random.fold_in(key, 11)
    second_key = jax.random.fold_in(key, 12)
    counts_drawn = jax.random.randint(first_key, (SECT,), B // 4, B + 1)
    chosen = jax.random.randint(second_key, (), 0, SECT)
    return jnp.where(jnp.arange(SECT) == chosen, B, counts_drawn).astype(jnp.int32)


def levels(key, shape, split, low, high):
    def one(position, parts):
        draws = jax.random.uniform(jax.random.fold_in(jax.random.fold_in(key, 6), position), (parts,), jnp.float32, low / len(split), high / len(split))
        return jnp.repeat(jnp.exp(draws), shape[position] // parts).reshape((-1,) + (1,) * (len(shape) - position - 1))

    level = one(*split[0])
    for cut in split[1:]:
        level = level * one(*cut)
    return level


def centred(stream_key, shape, deviation, reach, shards=(), kind=jnp.bfloat16):
    result = jax.random.normal(stream_key, shape, jnp.float32) * deviation
    if len(shards) > 0:
        result = levels(stream_key, shape, shards, -0.22, 0.18) * result
    return jnp.clip(result, min=-reach, max=reach).astype(kind)


def setup_inputs(seed: int = 0) -> dict:
    splits = jax.random.split(jax.random.key(seed), 7)
    return {
        "propagator": centred(splits[0], (SECT, TIMES, B, B), 1.0, 6.0, ((0, 4), (1, 8))),
        "rising_op": centred(splits[1], (SECT, B, B), B ** -0.5, 0.25, ((0, 4),)),
        "energies": jnp.clip(jnp.exp(math.log(40.0) - 4.3820266 * jax.random.uniform(splits[2], (SECT, B), jnp.float32) ** levels(splits[2], (SECT, B), ((0, 4),), -0.2, 0.2)), 0.5, 40.0),
        "hyb_particle": jnp.clip(jnp.exp(math.log(1.0) - 1.609438 * jax.random.uniform(splits[3], (TIMES,), jnp.float32) ** levels(splits[3], (TIMES,), ((0, 8),), -0.2, 0.2)), 0.2, 1.0),
        "hyb_hole": jnp.clip(jnp.exp(math.log(1.0) - 1.609438 * jax.random.uniform(splits[4], (TIMES,), jnp.float32) ** levels(splits[4], (TIMES,), ((0, 8),), -0.2, 0.2)), 0.2, 1.0),
        "sector_sizes": draw_sector_sizes(jax.random.fold_in(splits[6], 71), 0),
    }


def reference(propagator, rising_op, energies, hyb_particle, hyb_hole, sector_sizes):
    highest = lax.Precision.HIGHEST
    step_size = 1.0 / TIMES
    positions = jnp.arange(B, dtype=jnp.int32)
    live_mask = positions[None, :] < sector_sizes[:, None]
    square = live_mask[:, :, None] & live_mask[:, None, :]
    masked_prop = jnp.where(square[:, None], propagator, jnp.zeros((), propagator.dtype))
    operator_wide = rising_op.astype(jnp.float32)
    raised = jnp.einsum('sik,stkl->stil', operator_wide, masked_prop.astype(jnp.float32), precision=highest).astype(jnp.bfloat16)
    upward = jnp.einsum('stik,sjk->stij', raised.astype(jnp.float32), operator_wide, precision=highest).astype(jnp.bfloat16)
    from_below = jnp.concatenate([jnp.zeros_like(upward[:1]), upward[:-1]], 0)
    from_above = jnp.concatenate([masked_prop[1:], jnp.zeros_like(masked_prop[:1])], 0)
    lowered = jnp.einsum('ski,stkl->stil', operator_wide, from_above.astype(jnp.float32), precision=highest).astype(jnp.bfloat16)
    downward = jnp.einsum('stik,skl->stil', lowered.astype(jnp.float32), operator_wide, precision=highest)
    combined = hyb_particle[None, :, None, None] * from_below.astype(jnp.float32) + hyb_hole[None, :, None, None] * downward
    self_energy = jnp.where(square[:, None], combined, jnp.zeros((), jnp.float32)).astype(jnp.bfloat16)
    identity = positions[:, None] == positions[None, :]

    def one_sector(operands):
        lag_table, history, level_rates, live_row = operands
        lag_wide = lag_table.astype(jnp.float32)
        history_wide = history.astype(jnp.float32)
        running_sum = jnp.zeros((TIMES, B, B), jnp.float32)
        for lag in range(TIMES):
            running_sum = running_sum.at[lag:].add(jnp.einsum('ik,tkl->til', lag_wide[lag], history_wide[:TIMES - lag], precision=highest))
        convolved = step_size * running_sum
        decay = jnp.exp(-step_size * level_rates)

        def advance(running, term):
            running = decay[:, None] * running + term
            return running, running

        _, summed = lax.scan(advance, jnp.zeros((B, B), jnp.float32), convolved)
        moments = jnp.arange(TIMES).astype(jnp.float32)
        free_part = jnp.where(live_row[None, :], jnp.exp(-level_rates[None, :] * (moments[:, None] * step_size)), jnp.zeros((), jnp.float32))
        diagonal = jnp.where(identity[None], free_part[:, :, None], jnp.zeros((), jnp.float32))
        return (diagonal - step_size * summed).astype(jnp.bfloat16)

    return lax.map(one_sector, (self_energy, masked_prop, energies, live_mask))
```

```python
import functools
import jax
import jax.numpy as jnp
from jax import lax
from jax.experimental import pallas as pl
from jax.experimental.pallas import tpu as pltpu
from jax.sharding import PartitionSpec as P


def shifted(block, axis, distance):
    devices = range(lax.axis_size(axis))
    route = [(i - distance, i) for i in devices if i - distance in devices]
    return lax.ppermute(block, axis, route)


def general_device(propagator, rising_op, energies, hyb_particle, hyb_hole, sector_sizes):
    t_dev = propagator.shape[1]
    states = propagator.shape[2]
    time_count = t_dev * lax.axis_size("tm")
    step_size = 1.0 / time_count
    positions = jnp.arange(states, dtype=jnp.int32)
    live_mask = positions < sector_sizes[0]
    square = live_mask[:, None] & live_mask[None, :]
    masked_prop = jnp.where(square[None], propagator[0], jnp.zeros((), jnp.bfloat16))
    operator = rising_op[0]
    raised = jnp.einsum(
        "ik,tkl->til", operator, masked_prop, preferred_element_type=jnp.float32
    ).astype(jnp.bfloat16)
    upward = jnp.einsum("tik,jk->tij", raised, operator, preferred_element_type=jnp.float32).astype(
        jnp.bfloat16
    )
    from_below = shifted(upward, "sector", 1)
    from_above = shifted(masked_prop, "sector", -1)
    lowered = jnp.einsum(
        "ki,tkl->til", operator, from_above, preferred_element_type=jnp.float32
    ).astype(jnp.bfloat16)
    downward = jnp.einsum("tik,kl->til", lowered, operator, preferred_element_type=jnp.float32)
    combined = (
        hyb_particle[:, None, None] * from_below.astype(jnp.float32)
        + hyb_hole[:, None, None] * downward
    )
    self_energy = jnp.where(square[None], combined, jnp.zeros((), jnp.float32)).astype(jnp.bfloat16)
    rows_each = states // lax.axis_size("tm")
    first_row = lax.axis_index("tm") * rows_each
    lag_rows = lax.all_to_all(self_energy, "tm", split_axis=1, concat_axis=0, tiled=True)
    history = lax.all_gather(masked_prop, "tm", axis=0, tiled=True)
    mirrored = jnp.concatenate([history[::-1], history], 0)
    slots = jnp.arange(time_count, dtype=jnp.int32)
    wide_slots = jnp.arange(time_count + 1, dtype=jnp.int32)

    def pair_step(lag, sums):
        forward, backward = sums
        other = time_count - 1 - lag
        window = lax.dynamic_slice_in_dim(mirrored, lag, time_count + 1, 0)
        near = lax.dynamic_index_in_dim(lag_rows, lag, 0, keepdims=False)
        far = lax.dynamic_index_in_dim(lag_rows, other, 0, keepdims=False)
        left = jnp.where((wide_slots < time_count - lag)[:, None, None], near[None], far[None])
        product = jnp.einsum("uik,ukl->uil", left, window, preferred_element_type=jnp.float32)
        backward = backward + jnp.where(
            (slots < time_count - lag)[:, None, None],
            product[:time_count],
            jnp.zeros((), jnp.float32),
        )
        forward = forward + jnp.where(
            (slots >= time_count - lag - 1)[:, None, None], product[1:], jnp.zeros((), jnp.float32)
        )
        return (forward, backward)

    empty_rows = jnp.zeros((time_count, rows_each, states), jnp.float32)
    forward, backward = lax.fori_loop(0, time_count // 2, pair_step, (empty_rows, empty_rows))
    convolved = step_size * (forward + backward[::-1])
    row_ids = first_row + jnp.arange(rows_each, dtype=jnp.int32)
    row_rates = lax.dynamic_slice_in_dim(energies[0], first_row, rows_each, 0)
    decay_rows = jnp.exp(-step_size * row_rates)

    def advance(running, term):
        running = decay_rows[:, None] * running + term
        return (running, running)

    _, summed = lax.scan(advance, jnp.zeros((rows_each, states), jnp.float32), convolved)
    moments = jnp.arange(time_count).astype(jnp.float32) * step_size
    live_rows = row_ids < sector_sizes[0]
    free_part = jnp.where(
        live_rows[None, :],
        jnp.exp(-row_rates[None, :] * moments[:, None]),
        jnp.zeros((), jnp.float32),
    )
    diagonal = jnp.where(
        (row_ids[:, None] == positions[None, :])[None],
        free_part[:, :, None],
        jnp.zeros((), jnp.float32),
    )
    new_rows = (diagonal - step_size * summed).astype(jnp.bfloat16)
    return lax.all_to_all(new_rows, "tm", split_axis=0, concat_axis=1, tiled=True)[None]


MESH = pl.DeviceIdType.MESH
ROW_TILE = 16
LANES = 128
SUBLANES = 8
CORE, ACROSS, ALONG = 1, 2, 4
PIECES = 4
VMEM_GRANT = 211 * 2**18


def flipped(index, mask):
    bit = 1
    while bit <= mask:
        if mask & bit:
            index = index + bit - 2 * bit * lax.rem(lax.div(index, bit), 2)
        bit *= 2
    return index


def fused_kernel(
    times,
    sectors,
    size_hbm,
    particle_hbm,
    hole_hbm,
    prop_hbm,
    operator_hbm,
    energy_hbm,
    out_ref,
    size_ref,
    particle_ref,
    hole_ref,
    energy_ref,
    history,
    operator,
    raiser,
    turned,
    turned_in,
    pair,
    up_rows,
    down_rows,
    below,
    above,
    energy_in,
    sums,
    running,
    fresh,
    passing,
    strengths,
    load_sem,
    turned_send,
    turned_recv,
    up_send,
    up_recv,
    down_send,
    down_recv,
    piece_send,
    piece_recv,
    strength_send,
    strength_recv,
    out_send,
    out_recv,
    passing_send,
    passing_recv,
):
    states = prop_hbm.shape[-1]
    rows = states // times
    quarter = states // PIECES
    step_size = 1.0 / times
    me = lax.axis_index("tm")
    sector = lax.axis_index("sector")
    has_below = sector > 0
    has_above = sector < sectors - 1
    core = lax.rem(me, 2)
    even = me - core
    partner = flipped(me, CORE)
    x_even, y_even = flipped(even, ACROSS), flipped(even, ALONG)
    d_even = flipped(even, ACROSS | ALONG)

    loads = [
        pltpu.make_async_copy(src, dst, load_sem.at[i])
        for i, (src, dst) in enumerate(
            [
                (prop_hbm.at[0, 0], history.at[me]),
                (size_hbm, size_ref),
                (operator_hbm.at[0], operator),
                (particle_hbm, particle_ref),
                (hole_hbm, hole_ref),
                (energy_hbm, energy_ref),
            ]
        )
    ]
    barrier = pltpu.get_barrier_semaphore()
    for mask in range(1, times):
        pl.semaphore_signal(
            barrier, inc=1, device_id={"tm": flipped(me, mask)}, device_id_type=MESH
        )

    @pl.when(has_below)
    def _():
        pl.semaphore_signal(barrier, inc=1, device_id={"sector": sector - 1}, device_id_type=MESH)

    @pl.when(has_above)
    def _():
        pl.semaphore_signal(barrier, inc=1, device_id={"sector": sector + 1}, device_id_type=MESH)

    for load in loads:
        load.start()

    def row_block(index):
        return pl.ds(pl.multiple_of(index * rows, rows), rows)

    def piece_copy(step, time, q):
        piece = history.at[time, pl.ds(pl.multiple_of(q * quarter, quarter), quarter)]
        return pltpu.make_async_remote_copy(
            src_ref=piece,
            dst_ref=piece,
            send_sem=piece_send.at[step.bit_length() - 1, time, q],
            recv_sem=piece_recv.at[time, q],
            device_id={"tm": flipped(me, step)},
            device_id_type=MESH,
        )

    mine = [2 * core, 2 * core + 1]
    other = [2 - 2 * core, 3 - 2 * core]

    def turned_copy(step=1):
        return pltpu.make_async_remote_copy(
            src_ref=turned,
            dst_ref=turned_in,
            send_sem=turned_send,
            recv_sem=turned_recv,
            device_id={"sector": sector + step},
            device_id_type=MESH,
        )

    def up_copy(slot, time, step=1):
        block = row_block(time)
        return pltpu.make_async_remote_copy(
            src_ref=up_rows.at[block],
            dst_ref=below.at[block],
            send_sem=up_send.at[slot],
            recv_sem=up_recv.at[slot],
            device_id={"sector": sector + step},
            device_id_type=MESH,
        )

    def down_copy(slot, time, step=-1):
        block = row_block(time)
        return pltpu.make_async_remote_copy(
            src_ref=down_rows.at[block],
            dst_ref=above.at[block],
            send_sem=down_send.at[slot],
            recv_sem=down_recv.at[slot],
            device_id={"sector": sector + step},
            device_id_type=MESH,
        )

    def strength_copy(mask, block):
        return pltpu.make_async_remote_copy(
            src_ref=strengths.at[block],
            dst_ref=strengths.at[block],
            send_sem=strength_send.at[mask],
            recv_sem=strength_recv.at[mask],
            device_id={"tm": flipped(me, mask)},
            device_id_type=MESH,
        )

    def out_copy(moment, place):
        return pltpu.make_async_remote_copy(
            src_ref=fresh.at[moment],
            dst_ref=out_ref.at[0, 0, row_block(place)],
            send_sem=out_send.at[moment],
            recv_sem=out_recv.at[place],
            device_id={"tm": moment},
            device_id_type=MESH,
        )

    def passing_copy():
        return pltpu.make_async_remote_copy(
            src_ref=fresh.at[d_even],
            dst_ref=passing,
            send_sem=passing_send.at[0],
            recv_sem=passing_recv,
            device_id={"tm": flipped(me, ALONG)},
            device_id_type=MESH,
        )

    def passed_copy():
        return pltpu.make_async_remote_copy(
            src_ref=passing,
            dst_ref=out_ref.at[0, 0, row_block(flipped(me, ALONG))],
            send_sem=passing_send.at[1],
            recv_sem=out_recv.at[flipped(me, ALONG)],
            device_id={"tm": x_even},
            device_id_type=MESH,
        )

    loads[0].wait()
    for load in loads[3:]:
        load.wait()
    first_line = lax.broadcasted_iota(jnp.int32, strengths.shape[1:], 0) == 0
    strengths[me] = jnp.where(first_line, particle_ref[0], hole_ref[0])
    neighbours = jnp.where(has_below, 1, 0) + jnp.where(has_above, 1, 0)
    pl.semaphore_wait(barrier, times - 1 + neighbours)

    def links_start(time):
        for step, r in ((ACROSS, 0), (ALONG, 1), (ACROSS, 1), (ALONG, 0)):
            piece_copy(step, time, mine[r]).start()

    for mask in range(1, times):
        strength_copy(mask, me).start()
    for q in other:
        piece_copy(CORE, me, q).start()

    @pl.when(core == 0)
    def _():
        links_start(me)

    for q in mine:
        piece_copy(CORE, me, q).start()
    loads[2].wait()
    row_ids = me * rows + lax.broadcasted_iota(jnp.int32, (rows, states), 0)
    column_ids = lax.broadcasted_iota(jnp.int32, (rows, states), 1)
    on_diagonal = row_ids == column_ids
    chosen = jnp.where(on_diagonal, 1.0, 0.0).astype(jnp.bfloat16)
    turned[...] = lax.dot_general(
        chosen, operator[...], (((1,), (1,)), ((), ())), preferred_element_type=jnp.float32
    ).astype(jnp.bfloat16)

    @pl.when(has_above)
    def _():
        turned_copy().start()

    loads[1].wait()
    size = size_ref[0]
    live_columns = lax.broadcasted_iota(jnp.int32, (states, states), 1) < size
    live_line = column_ids < size
    raiser[...] = jnp.where(live_columns, operator[...].astype(jnp.float32), 0.0).astype(
        jnp.bfloat16
    )
    for q in mine:
        piece_copy(CORE, partner, q).wait_recv()

    links_start(partner)

    @pl.when(core == 1)
    def _():
        links_start(me)

    def product_of(left, time):
        return jnp.dot(left, history[time], preferred_element_type=jnp.float32)

    def send_up(slot, time, raised):
        up_rows[row_block(time)] = lax.dot_general(
            raised.astype(jnp.bfloat16),
            raiser[...],
            (((1,), (1,)), ((), ())),
            preferred_element_type=jnp.float32,
        ).astype(jnp.bfloat16)

        @pl.when(has_above)
        def _():
            up_copy(slot, time).start()

    def send_down(slot, time, lowered):
        down_rows[row_block(time)] = jnp.where(live_line, lowered, 0.0).astype(jnp.bfloat16)

        @pl.when(has_below)
        def _():
            down_copy(slot, time).start()

    def arrive(step, time, r):
        piece_copy(step, time, mine[r]).wait_recv()
        piece_copy(CORE, time, mine[r]).start()

    def relay(step, time, r):
        piece_copy(step, time, mine[r]).start()

    def shared(time):
        for q in other:
            piece_copy(CORE, time, q).wait_recv()

    order = [me, partner, x_even, y_even, x_even + 1, y_even + 1, d_even, d_even + 1]
    last = order[-1]

    pair[0:rows] = raiser[row_block(me)]
    send_up(0, me, product_of(pair[0:rows], me))
    shared(partner)
    send_up(1, partner, product_of(pair[0:rows], partner))

    rates = jnp.sum(
        jnp.where(on_diagonal, energy_ref[...], jnp.zeros((), jnp.float32)), axis=1, keepdims=True
    )
    decay = jnp.exp(-step_size * rates)
    running[...] = jnp.zeros_like(running)
    sums[...] = jnp.zeros_like(sums)

    @pl.when(jnp.logical_not(has_below))
    def _():
        turned_in[...] = jnp.zeros_like(turned_in)
        below[...] = jnp.zeros_like(below)

    @pl.when(jnp.logical_not(has_above))
    def _():
        above[...] = jnp.zeros_like(above)

    arrive(ACROSS, x_even, 0)
    relay(ALONG, x_even, 0)
    arrive(ALONG, y_even, 1)
    relay(ACROSS, y_even, 1)

    @pl.when(has_below)
    def _():
        turned_copy(-1).wait_recv()

    pair[rows : 2 * rows] = jnp.where(
        live_line, turned_in[...].astype(jnp.float32), 0.0
    ).astype(jnp.bfloat16)
    for slot in range(2):
        send_down(slot, order[slot], product_of(pair[rows : 2 * rows], order[slot]))

    arrive(ACROSS, x_even, 1)
    arrive(ALONG, y_even, 0)

    def both(slot):
        time = order[slot]
        shared(time)
        result = product_of(pair[...], time)
        send_down(slot, time, result[rows : 2 * rows])
        send_up(slot, time, result[0:rows])

    live_rows = (row_ids < size) & (column_ids < size)
    shown = on_diagonal & (row_ids < size)

    def combine(*slots):
        places = [row_block(order[slot]) for slot in slots]

        @pl.when(has_below)
        def _():
            for slot in slots:
                up_copy(slot, order[slot], -1).wait_recv()

        @pl.when(has_above)
        def _():
            for slot in slots:
                down_copy(slot, order[slot], 1).wait_recv()

        lowered = jnp.concatenate([above[place] for place in places], 0)
        downward = jnp.dot(lowered, operator[...], preferred_element_type=jnp.float32)
        for i, (slot, place) in enumerate(zip(slots, places)):
            level = strengths[order[slot]]
            combined = (
                level[0:1, 0:1] * below[place].astype(jnp.float32)
                + level[1:2, 0:1] * downward[i * rows : (i + 1) * rows]
            )
            energy_in[place] = jnp.where(live_rows, combined, jnp.zeros((), jnp.float32)).astype(
                jnp.bfloat16
            )

    def convolve(lag_even, *times_in):
        for time in times_in:

            @pl.when(lag_even + time < times)
            def _():
                left = energy_in[pl.ds(pl.multiple_of(lag_even * rows, rows), 2 * rows)]
                first = pl.multiple_of((lag_even + time) * rows, rows)
                sums[pl.ds(first, 2 * rows)] += jnp.dot(
                    left, history[time], preferred_element_type=jnp.float32
                )

    def finish(moment):
        place = row_block(moment)
        value = decay * running[...] + step_size * sums[place]
        running[...] = value
        instant = jnp.asarray(moment, jnp.int32).astype(jnp.float32) * step_size
        free_part = jnp.where(shown, jnp.exp(-rates * instant), jnp.zeros((), jnp.float32))
        fresh[moment] = jnp.where(
            live_rows, free_part - step_size * value, jnp.zeros((), jnp.float32)
        ).astype(jnp.bfloat16)

        @pl.when((me != moment) & (d_even != moment))
        def _():
            out_copy(moment, me).start()

        @pl.when(d_even == moment)
        def _():
            passing_copy().start()

        @pl.when(me == moment)
        def _():
            out_ref[0, 0, row_block(me)] = fresh[moment]

    x_odd, y_odd = x_even + 1, y_even + 1
    for mask in range(1, times):
        strength_copy(mask, flipped(me, mask)).wait_recv()
    both(2)
    both(3)
    combine(0, 1)
    convolve(even, even, even + 1)
    arrive(ACROSS, x_odd, 0)
    relay(ALONG, x_odd, 0)
    arrive(ALONG, y_odd, 1)
    relay(ACROSS, y_odd, 1)
    convolve(even, x_even, y_even)
    arrive(ACROSS, x_odd, 1)
    arrive(ALONG, y_odd, 0)
    combine(2, 3)
    both(4)
    both(5)
    arrive(ALONG, d_even, 0)
    arrive(ACROSS, d_even, 1)
    convolve(even, x_odd, y_odd)
    both(6)
    convolve(even, d_even)
    arrive(ALONG, last, 0)
    arrive(ACROSS, last, 1)
    combine(4, 5)
    convolve(x_even, y_even, y_odd)
    both(7)
    convolve(y_even, x_even, x_odd)
    convolve(x_even, even, even + 1, x_even, x_odd)
    convolve(y_even, even, even + 1, y_even, y_odd)
    for moment in range(times):

        @pl.when(moment < d_even)
        def _():
            finish(moment)

    convolve(even, last)
    convolve(x_even, d_even, last)
    convolve(y_even, d_even, last)
    combine(6, 7)
    for moment in range(times):
        convolve(d_even, moment)

        @pl.when(d_even + moment < times)
        def _():
            finish(d_even + moment)

    passing_copy().wait_recv()
    passed_copy().start()
    for mask in range(1, times):
        pltpu.make_async_remote_copy(
            src_ref=fresh.at[0],
            dst_ref=out_ref.at[0, 0, row_block(flipped(me, mask))],
            send_sem=out_send.at[0],
            recv_sem=out_recv.at[flipped(me, mask)],
            device_id={"tm": flipped(me, mask)},
            device_id_type=MESH,
        ).wait_recv()
    for moment in range(times):

        @pl.when((me != moment) & (d_even != moment))
        def _():
            out_copy(moment, me).wait_send()

    passing_copy().wait_send()
    passed_copy().wait_send()
    for mask in range(1, times):
        strength_copy(mask, me).wait_send()
    for q in mine + other:
        piece_copy(CORE, me, q).wait_send()
    for time in (even, even + 1):
        for step in (ACROSS, ALONG):
            for q in mine:
                piece_copy(step, time, q).wait_send()
    for parity in range(2):
        for base in (x_even, y_even, d_even):
            for q in mine:
                piece_copy(CORE, base + parity, q).wait_send()
        piece_copy(ALONG, x_even + parity, mine[0]).wait_send()
        piece_copy(ACROSS, y_even + parity, mine[1]).wait_send()

    @pl.when(has_below)
    def _():
        for slot in range(times):
            down_copy(slot, order[slot]).wait_send()

    @pl.when(has_above)
    def _():
        turned_copy().wait_send()
        for slot in range(times):
            up_copy(slot, order[slot]).wait_send()


def fused_device(propagator, rising_op, energies, hyb_particle, hyb_hole, sector_sizes):
    times = lax.axis_size("tm")
    states = propagator.shape[-1]
    rows = states // times
    square = (states, states)
    narrow, wide = jnp.bfloat16, jnp.float32
    anywhere = pl.BlockSpec(memory_space=pltpu.HBM)
    dma = pltpu.SemaphoreType.DMA
    return pl.pallas_call(
        functools.partial(fused_kernel, times, lax.axis_size("sector")),
        out_shape=jax.ShapeDtypeStruct(propagator.shape, narrow),
        in_specs=[anywhere] * 6,
        out_specs=pl.BlockSpec(memory_space=pltpu.VMEM),
        scratch_shapes=[
            pltpu.SMEM((1,), jnp.int32),
            pltpu.SMEM((1,), wide),
            pltpu.SMEM((1,), wide),
            pltpu.VMEM(energies.shape, wide),
            pltpu.VMEM((times,) + square, narrow),
            pltpu.VMEM(square, narrow),
            pltpu.VMEM(square, narrow),
            pltpu.VMEM((rows, states), narrow),
            pltpu.VMEM((rows, states), narrow),
            pltpu.VMEM((2 * rows, states), narrow),
            pltpu.VMEM(square, narrow),
            pltpu.VMEM(square, narrow),
            pltpu.VMEM(square, narrow),
            pltpu.VMEM(square, narrow),
            pltpu.VMEM(square, narrow),
            pltpu.VMEM((states + rows, states), wide),
            pltpu.VMEM((rows, states), wide),
            pltpu.VMEM((times, rows, states), narrow),
            pltpu.VMEM((rows, states), narrow),
            pltpu.VMEM((times, SUBLANES, LANES), wide),
            dma((6,)),
            dma,
            dma,
            dma((times,)),
            dma((times,)),
            dma((times,)),
            dma((times,)),
            dma((3, times, PIECES)),
            dma((times, PIECES)),
            dma((times,)),
            dma((times,)),
            dma((times,)),
            dma((times,)),
            dma((2,)),
            dma,
        ],
        compiler_params=pltpu.CompilerParams(
            collective_id=0, has_side_effects=True, vmem_limit_bytes=VMEM_GRANT
        ),
    )(sector_sizes, hyb_particle, hyb_hole, propagator, rising_op, energies)


def per_device(propagator, rising_op, energies, hyb_particle, hyb_hole, sector_sizes):
    times = lax.axis_size("tm")
    states = propagator.shape[-1]
    fits = (
        propagator.shape[1] == 1
        and times == (CORE | ACROSS | ALONG) + 1
        and states % (times * ROW_TILE) == 0
        and states % (PIECES * ROW_TILE) == 0
        and states % LANES == 0
    )
    chosen = fused_device if fits else general_device
    return chosen(propagator, rising_op, energies, hyb_particle, hyb_hole, sector_sizes)


def solution(mesh):
    placed = (
        P("sector", "tm", None, None),
        P("sector", None, None),
        P("sector", None),
        P("tm"),
        P("tm"),
        P("sector"),
    )
    return jax.shard_map(
        per_device,
        mesh=mesh,
        in_specs=placed,
        out_specs=P("sector", "tm", None, None),
        check_vma=False,
    )
```

```python
import functools
import jax
import jax.numpy as jnp
from jax import lax
from jax.experimental import pallas as pl
from jax.experimental.pallas import tpu as pltpu
from jax.sharding import PartitionSpec as P


def shifted(block, axis, distance):
    devices = range(lax.axis_size(axis))
    route = [(i - distance, i) for i in devices if i - distance in devices]
    return lax.ppermute(block, axis, route)


def general_device(propagator, rising_op, energies, hyb_particle, hyb_hole, sector_sizes):
    t_dev = propagator.shape[1]
    states = propagator.shape[2]
    time_count = t_dev * lax.axis_size("tm")
    step_size = 1.0 / time_count
    positions = jnp.arange(states, dtype=jnp.int32)
    live_mask = positions < sector_sizes[0]
    square = live_mask[:, None] & live_mask[None, :]
    masked_prop = jnp.where(square[None], propagator[0], jnp.zeros((), jnp.bfloat16))
    operator = rising_op[0]
    raised = jnp.einsum(
        "ik,tkl->til", operator, masked_prop, preferred_element_type=jnp.float32
    ).astype(jnp.bfloat16)
    upward = jnp.einsum("tik,jk->tij", raised, operator, preferred_element_type=jnp.float32).astype(
        jnp.bfloat16
    )
    from_below = shifted(upward, "sector", 1)
    from_above = shifted(masked_prop, "sector", -1)
    lowered = jnp.einsum(
        "ki,tkl->til", operator, from_above, preferred_element_type=jnp.float32
    ).astype(jnp.bfloat16)
    downward = jnp.einsum("tik,kl->til", lowered, operator, preferred_element_type=jnp.float32)
    combined = (
        hyb_particle[:, None, None] * from_below.astype(jnp.float32)
        + hyb_hole[:, None, None] * downward
    )
    self_energy = jnp.where(square[None], combined, jnp.zeros((), jnp.float32)).astype(jnp.bfloat16)
    rows_each = states // lax.axis_size("tm")
    first_row = lax.axis_index("tm") * rows_each
    lag_rows = lax.all_to_all(self_energy, "tm", split_axis=1, concat_axis=0, tiled=True)
    history = lax.all_gather(masked_prop, "tm", axis=0, tiled=True)
    mirrored = jnp.concatenate([history[::-1], history], 0)
    slots = jnp.arange(time_count, dtype=jnp.int32)
    wide_slots = jnp.arange(time_count + 1, dtype=jnp.int32)

    def pair_step(lag, sums):
        forward, backward = sums
        other = time_count - 1 - lag
        window = lax.dynamic_slice_in_dim(mirrored, lag, time_count + 1, 0)
        near = lax.dynamic_index_in_dim(lag_rows, lag, 0, keepdims=False)
        far = lax.dynamic_index_in_dim(lag_rows, other, 0, keepdims=False)
        left = jnp.where((wide_slots < time_count - lag)[:, None, None], near[None], far[None])
        product = jnp.einsum("uik,ukl->uil", left, window, preferred_element_type=jnp.float32)
        backward = backward + jnp.where(
            (slots < time_count - lag)[:, None, None],
            product[:time_count],
            jnp.zeros((), jnp.float32),
        )
        forward = forward + jnp.where(
            (slots >= time_count - lag - 1)[:, None, None], product[1:], jnp.zeros((), jnp.float32)
        )
        return (forward, backward)

    empty_rows = jnp.zeros((time_count, rows_each, states), jnp.float32)
    forward, backward = lax.fori_loop(0, time_count // 2, pair_step, (empty_rows, empty_rows))
    convolved = step_size * (forward + backward[::-1])
    row_ids = first_row + jnp.arange(rows_each, dtype=jnp.int32)
    row_rates = lax.dynamic_slice_in_dim(energies[0], first_row, rows_each, 0)
    decay_rows = jnp.exp(-step_size * row_rates)

    def advance(running, term):
        running = decay_rows[:, None] * running + term
        return (running, running)

    _, summed = lax.scan(advance, jnp.zeros((rows_each, states), jnp.float32), convolved)
    moments = jnp.arange(time_count).astype(jnp.float32) * step_size
    live_rows = row_ids < sector_sizes[0]
    free_part = jnp.where(
        live_rows[None, :],
        jnp.exp(-row_rates[None, :] * moments[:, None]),
        jnp.zeros((), jnp.float32),
    )
    diagonal = jnp.where(
        (row_ids[:, None] == positions[None, :])[None],
        free_part[:, :, None],
        jnp.zeros((), jnp.float32),
    )
    new_rows = (diagonal - step_size * summed).astype(jnp.bfloat16)
    return lax.all_to_all(new_rows, "tm", split_axis=0, concat_axis=1, tiled=True)[None]


MESH = pl.DeviceIdType.MESH
ROW_TILE = 16
LANES = 128
SUBLANES = 8
CORE, ACROSS, ALONG = 1, 2, 4
PIECES = 4
VMEM_GRANT = 211 * 2**18


def flipped(index, mask):
    bit = 1
    while bit <= mask:
        if mask & bit:
            index = index + bit - 2 * bit * lax.rem(lax.div(index, bit), 2)
        bit *= 2
    return index


def fused_kernel(
    times,
    sectors,
    size_hbm,
    particle_hbm,
    hole_hbm,
    prop_hbm,
    operator_hbm,
    energy_hbm,
    out_ref,
    size_ref,
    particle_ref,
    hole_ref,
    energy_ref,
    history,
    operator,
    raiser,
    raiser_turned,
    turned,
    turned_in,
    pair,
    up_rows,
    down_rows,
    below,
    above,
    energy_in,
    sums,
    running,
    fresh,
    strengths,
    load_sem,
    turned_send,
    turned_recv,
    up_send,
    up_recv,
    down_send,
    down_recv,
    piece_send,
    piece_recv,
    strength_send,
    strength_recv,
    out_send,
    out_recv,
):
    states = prop_hbm.shape[-1]
    rows = states // times
    quarter = states // PIECES
    step_size = 1.0 / times
    me = lax.axis_index("tm")
    sector = lax.axis_index("sector")
    has_below = sector > 0
    has_above = sector < sectors - 1
    core = lax.rem(me, 2)
    even = me - core
    partner = flipped(me, CORE)
    x_even, y_even = flipped(even, ACROSS), flipped(even, ALONG)
    d_even = flipped(even, ACROSS | ALONG)

    loads = [
        pltpu.make_async_copy(src, dst, load_sem.at[i])
        for i, (src, dst) in enumerate(
            [
                (prop_hbm.at[0, 0], history.at[me]),
                (size_hbm, size_ref),
                (operator_hbm.at[0], operator),
                (particle_hbm, particle_ref),
                (hole_hbm, hole_ref),
                (energy_hbm, energy_ref),
            ]
        )
    ]
    barrier = pltpu.get_barrier_semaphore()
    for mask in range(1, times):
        pl.semaphore_signal(
            barrier, inc=1, device_id={"tm": flipped(me, mask)}, device_id_type=MESH
        )

    @pl.when(has_below)
    def _():
        pl.semaphore_signal(barrier, inc=1, device_id={"sector": sector - 1}, device_id_type=MESH)

    @pl.when(has_above)
    def _():
        pl.semaphore_signal(barrier, inc=1, device_id={"sector": sector + 1}, device_id_type=MESH)

    for load in loads:
        load.start()

    def row_block(index):
        return pl.ds(pl.multiple_of(index * rows, rows), rows)

    def piece_copy(step, time, q):
        piece = history.at[time, pl.ds(pl.multiple_of(q * quarter, quarter), quarter)]
        return pltpu.make_async_remote_copy(
            src_ref=piece,
            dst_ref=piece,
            send_sem=piece_send.at[step.bit_length() - 1, time, q],
            recv_sem=piece_recv.at[time, q],
            device_id={"tm": flipped(me, step)},
            device_id_type=MESH,
        )

    mine = [2 * core, 2 * core + 1]
    other = [2 - 2 * core, 3 - 2 * core]

    def turned_copy(step=1):
        return pltpu.make_async_remote_copy(
            src_ref=turned,
            dst_ref=turned_in,
            send_sem=turned_send,
            recv_sem=turned_recv,
            device_id={"sector": sector + step},
            device_id_type=MESH,
        )

    def up_copy(slot, time, step=1):
        block = row_block(time)
        return pltpu.make_async_remote_copy(
            src_ref=up_rows.at[block],
            dst_ref=below.at[block],
            send_sem=up_send.at[slot],
            recv_sem=up_recv.at[slot],
            device_id={"sector": sector + step},
            device_id_type=MESH,
        )

    def down_copy(slot, time, step=-1):
        block = row_block(time)
        return pltpu.make_async_remote_copy(
            src_ref=down_rows.at[block],
            dst_ref=above.at[block],
            send_sem=down_send.at[slot],
            recv_sem=down_recv.at[slot],
            device_id={"sector": sector + step},
            device_id_type=MESH,
        )

    def strength_copy(mask, block):
        return pltpu.make_async_remote_copy(
            src_ref=strengths.at[block],
            dst_ref=strengths.at[block],
            send_sem=strength_send.at[mask],
            recv_sem=strength_recv.at[mask],
            device_id={"tm": flipped(me, mask)},
            device_id_type=MESH,
        )

    def out_copy(moment, place):
        return pltpu.make_async_remote_copy(
            src_ref=fresh.at[moment],
            dst_ref=out_ref.at[0, 0, row_block(place)],
            send_sem=out_send.at[moment],
            recv_sem=out_recv.at[place],
            device_id={"tm": moment},
            device_id_type=MESH,
        )

    loads[0].wait()
    for load in loads[3:]:
        load.wait()
    first_line = lax.broadcasted_iota(jnp.int32, strengths.shape[1:], 0) == 0
    strengths[me] = jnp.where(first_line, particle_ref[0], hole_ref[0])
    neighbours = jnp.where(has_below, 1, 0) + jnp.where(has_above, 1, 0)
    pl.semaphore_wait(barrier, times - 1 + neighbours)

    def links_start(time):
        for step, r in ((ACROSS, 0), (ALONG, 1), (ACROSS, 1), (ALONG, 0)):
            piece_copy(step, time, mine[r]).start()

    for mask in range(1, times):
        strength_copy(mask, me).start()
    for q in other:
        piece_copy(CORE, me, q).start()

    @pl.when(core == 0)
    def _():
        links_start(me)

    for q in mine:
        piece_copy(CORE, me, q).start()
    loads[2].wait()
    row_ids = me * rows + lax.broadcasted_iota(jnp.int32, (rows, states), 0)
    column_ids = lax.broadcasted_iota(jnp.int32, (rows, states), 1)
    on_diagonal = row_ids == column_ids
    chosen = jnp.where(on_diagonal, 1.0, 0.0).astype(jnp.bfloat16)
    turned[...] = lax.dot_general(
        chosen, operator[...], (((1,), (1,)), ((), ())), preferred_element_type=jnp.float32
    ).astype(jnp.bfloat16)

    @pl.when(has_above)
    def _():
        turned_copy().start()

    loads[1].wait()
    size = size_ref[0]
    live_columns = lax.broadcasted_iota(jnp.int32, (states, states), 1) < size
    live_line = column_ids < size
    raiser[...] = jnp.where(live_columns, operator[...].astype(jnp.float32), 0.0).astype(
        jnp.bfloat16
    )
    for q in mine:
        piece_copy(CORE, partner, q).wait_recv()

    links_start(partner)

    @pl.when(core == 1)
    def _():
        links_start(me)

    def product_of(left, time):
        return jnp.dot(left, history[time], preferred_element_type=jnp.float32)

    def send_up(slot, time, raised):
        up_rows[row_block(time)] = jnp.dot(
            raised.astype(jnp.bfloat16), raiser_turned[...], preferred_element_type=jnp.float32
        ).astype(jnp.bfloat16)

        @pl.when(has_above)
        def _():
            up_copy(slot, time).start()

    def send_down(slot, time, lowered):
        down_rows[row_block(time)] = jnp.where(live_line, lowered, 0.0).astype(jnp.bfloat16)

        @pl.when(has_below)
        def _():
            down_copy(slot, time).start()

    def arrive(step, time, r):
        piece_copy(step, time, mine[r]).wait_recv()
        piece_copy(CORE, time, mine[r]).start()

    def relay(step, time, r):
        piece_copy(step, time, mine[r]).start()

    def shared(time):
        for q in other:
            piece_copy(CORE, time, q).wait_recv()

    order = [me, partner, x_even, y_even, x_even + 1, y_even + 1, d_even, d_even + 1]
    last = order[-1]

    pair[0:rows] = raiser[row_block(me)]
    raiser_turned[...] = raiser[...].T
    send_up(0, me, product_of(pair[0:rows], me))
    shared(partner)
    send_up(1, partner, product_of(pair[0:rows], partner))

    rates = jnp.sum(
        jnp.where(on_diagonal, energy_ref[...], jnp.zeros((), jnp.float32)), axis=1, keepdims=True
    )
    decay = jnp.exp(-step_size * rates)
    running[...] = jnp.zeros_like(running)
    sums[...] = jnp.zeros_like(sums)

    @pl.when(jnp.logical_not(has_below))
    def _():
        turned_in[...] = jnp.zeros_like(turned_in)
        below[...] = jnp.zeros_like(below)

    @pl.when(jnp.logical_not(has_above))
    def _():
        above[...] = jnp.zeros_like(above)

    arrive(ACROSS, x_even, 0)
    relay(ALONG, x_even, 0)
    arrive(ALONG, y_even, 1)
    relay(ACROSS, y_even, 1)

    @pl.when(has_below)
    def _():
        turned_copy(-1).wait_recv()

    pair[rows : 2 * rows] = jnp.where(
        live_line, turned_in[...].astype(jnp.float32), 0.0
    ).astype(jnp.bfloat16)
    for slot in range(2):
        send_down(slot, order[slot], product_of(pair[rows : 2 * rows], order[slot]))

    arrive(ACROSS, x_even, 1)
    arrive(ALONG, y_even, 0)

    def both(slot):
        time = order[slot]
        shared(time)
        result = product_of(pair[...], time)
        send_down(slot, time, result[rows : 2 * rows])
        send_up(slot, time, result[0:rows])

    live_rows = (row_ids < size) & (column_ids < size)
    shown = on_diagonal & (row_ids < size)

    def combine(*slots):
        places = [row_block(order[slot]) for slot in slots]

        @pl.when(has_below)
        def _():
            for slot in slots:
                up_copy(slot, order[slot], -1).wait_recv()

        @pl.when(has_above)
        def _():
            for slot in slots:
                down_copy(slot, order[slot], 1).wait_recv()

        lowered = jnp.concatenate([above[place] for place in places], 0)
        downward = jnp.dot(lowered, operator[...], preferred_element_type=jnp.float32)
        for i, (slot, place) in enumerate(zip(slots, places)):
            level = strengths[order[slot]]
            combined = (
                level[0:1, 0:1] * below[place].astype(jnp.float32)
                + level[1:2, 0:1] * downward[i * rows : (i + 1) * rows]
            )
            energy_in[place] = jnp.where(live_rows, combined, jnp.zeros((), jnp.float32)).astype(
                jnp.bfloat16
            )

    def accumulate(lag_even, *bases):
        left = energy_in[pl.ds(pl.multiple_of(lag_even * rows, rows), 2 * rows)]
        for base in bases:
            first = pl.multiple_of((lag_even + base) * rows, rows)
            sums[pl.ds(first, 2 * rows)] += jnp.dot(
                left, history[base], preferred_element_type=jnp.float32
            )

    def convolve(lag_even, *bases):
        @pl.when(lag_even + bases[0] < times)
        def _():
            accumulate(lag_even, *bases)

    def finish(moment):
        place = row_block(moment)
        value = decay * running[...] + step_size * sums[place]
        running[...] = value
        instant = jnp.asarray(moment, jnp.int32).astype(jnp.float32) * step_size
        free_part = jnp.where(shown, jnp.exp(-rates * instant), jnp.zeros((), jnp.float32))
        fresh[moment] = jnp.where(
            live_rows, free_part - step_size * value, jnp.zeros((), jnp.float32)
        ).astype(jnp.bfloat16)

        @pl.when((me != moment))
        def _():
            out_copy(moment, me).start()

        @pl.when(me == moment)
        def _():
            out_ref[0, 0, row_block(me)] = fresh[moment]

    x_odd, y_odd = x_even + 1, y_even + 1
    for mask in range(1, times):
        strength_copy(mask, flipped(me, mask)).wait_recv()
    both(2)
    both(3)
    combine(0, 1)
    convolve(even, even, even + 1)
    arrive(ACROSS, x_odd, 0)
    relay(ALONG, x_odd, 0)
    arrive(ALONG, y_odd, 1)
    relay(ACROSS, y_odd, 1)
    convolve(even, x_even)
    convolve(even, y_even)
    arrive(ACROSS, x_odd, 1)
    arrive(ALONG, y_odd, 0)
    combine(2, 3)
    both(4)
    both(5)
    arrive(ALONG, d_even, 0)
    arrive(ACROSS, d_even, 1)
    convolve(even, x_odd)
    convolve(even, y_odd)
    both(6)
    accumulate(even, d_even)
    arrive(ALONG, last, 0)
    arrive(ACROSS, last, 1)
    combine(4, 5)

    def finish_between(start, stop, allowed):
        for moment in range(start, stop, 2):

            @pl.when(allowed & (moment < d_even))
            def _():
                finish(moment)
                finish(moment + 1)

    first_half = d_even >= times // 2
    convolve(x_even, even, even + 1)
    convolve(x_even, x_even, x_odd)
    finish_between(0, times // 2, first_half)
    convolve(y_even, y_even, y_odd)
    finish_between(0, times // 2, jnp.logical_not(first_half))
    both(7)
    accumulate(x_even, y_even, y_odd)
    accumulate(y_even, x_even, x_odd)
    convolve(y_even, even, even + 1)
    finish_between(times // 2, times, first_half)
    accumulate(even, last)
    convolve(x_even, d_even, last)
    convolve(y_even, d_even, last)
    combine(6)
    sums[row_block(d_even)] += jnp.dot(
        energy_in[row_block(d_even)], history[0], preferred_element_type=jnp.float32
    )
    finish(d_even)
    combine(7)
    for moment in range(0, times, 2):

        @pl.when(d_even + moment < times)
        def _():
            accumulate(d_even, moment, moment + 1)
            if moment > 0:
                finish(d_even + moment)
            finish(d_even + moment + 1)

    for mask in range(1, times):
        pltpu.make_async_remote_copy(
            src_ref=fresh.at[0],
            dst_ref=out_ref.at[0, 0, row_block(flipped(me, mask))],
            send_sem=out_send.at[0],
            recv_sem=out_recv.at[flipped(me, mask)],
            device_id={"tm": flipped(me, mask)},
            device_id_type=MESH,
        ).wait_recv()
    for moment in range(times):

        @pl.when((me != moment))
        def _():
            out_copy(moment, me).wait_send()

    for mask in range(1, times):
        strength_copy(mask, me).wait_send()
    for q in mine + other:
        piece_copy(CORE, me, q).wait_send()
    for time in (even, even + 1):
        for step in (ACROSS, ALONG):
            for q in mine:
                piece_copy(step, time, q).wait_send()
    for parity in range(2):
        for base in (x_even, y_even, d_even):
            for q in mine:
                piece_copy(CORE, base + parity, q).wait_send()
        piece_copy(ALONG, x_even + parity, mine[0]).wait_send()
        piece_copy(ACROSS, y_even + parity, mine[1]).wait_send()

    @pl.when(has_below)
    def _():
        for slot in range(times):
            down_copy(slot, order[slot]).wait_send()

    @pl.when(has_above)
    def _():
        turned_copy().wait_send()
        for slot in range(times):
            up_copy(slot, order[slot]).wait_send()


def fused_device(propagator, rising_op, energies, hyb_particle, hyb_hole, sector_sizes):
    times = lax.axis_size("tm")
    states = propagator.shape[-1]
    rows = states // times
    square = (states, states)
    narrow, wide = jnp.bfloat16, jnp.float32
    anywhere = pl.BlockSpec(memory_space=pltpu.HBM)
    dma = pltpu.SemaphoreType.DMA
    return pl.pallas_call(
        functools.partial(fused_kernel, times, lax.axis_size("sector")),
        out_shape=jax.ShapeDtypeStruct(propagator.shape, narrow),
        in_specs=[anywhere] * 6,
        out_specs=pl.BlockSpec(memory_space=pltpu.VMEM),
        scratch_shapes=[
            pltpu.SMEM((1,), jnp.int32),
            pltpu.SMEM((1,), wide),
            pltpu.SMEM((1,), wide),
            pltpu.VMEM(energies.shape, wide),
            pltpu.VMEM((times,) + square, narrow),
            pltpu.VMEM(square, narrow),
            pltpu.VMEM(square, narrow),
            pltpu.VMEM(square, narrow),
            pltpu.VMEM((rows, states), narrow),
            pltpu.VMEM((rows, states), narrow),
            pltpu.VMEM((2 * rows, states), narrow),
            pltpu.VMEM(square, narrow),
            pltpu.VMEM(square, narrow),
            pltpu.VMEM(square, narrow),
            pltpu.VMEM(square, narrow),
            pltpu.VMEM(square, narrow),
            pltpu.VMEM((states + rows, states), wide),
            pltpu.VMEM((rows, states), wide),
            pltpu.VMEM((times, rows, states), narrow),
            pltpu.VMEM((times, SUBLANES, LANES), wide),
            dma((6,)),
            dma,
            dma,
            dma((times,)),
            dma((times,)),
            dma((times,)),
            dma((times,)),
            dma((3, times, PIECES)),
            dma((times, PIECES)),
            dma((times,)),
            dma((times,)),
            dma((times,)),
            dma((times,)),
        ],
        compiler_params=pltpu.CompilerParams(
            collective_id=0, has_side_effects=True, vmem_limit_bytes=VMEM_GRANT
        ),
    )(sector_sizes, hyb_particle, hyb_hole, propagator, rising_op, energies)


def per_device(propagator, rising_op, energies, hyb_particle, hyb_hole, sector_sizes):
    times = lax.axis_size("tm")
    states = propagator.shape[-1]
    fits = (
        propagator.shape[1] == 1
        and times == (CORE | ACROSS | ALONG) + 1
        and states % (times * ROW_TILE) == 0
        and states % (PIECES * ROW_TILE) == 0
        and states % LANES == 0
    )
    chosen = fused_device if fits else general_device
    return chosen(propagator, rising_op, energies, hyb_particle, hyb_hole, sector_sizes)


def solution(mesh):
    placed = (
        P("sector", "tm", None, None),
        P("sector", None, None),
        P("sector", None),
        P("tm"),
        P("tm"),
        P("sector"),
    )
    return jax.shard_map(
        per_device,
        mesh=mesh,
        in_specs=placed,
        out_specs=P("sector", "tm", None, None),
        check_vma=False,
    )
```

```python
import functools
import jax
import jax.numpy as jnp
from jax import lax
from jax.experimental import pallas as pl
from jax.experimental.pallas import tpu as pltpu
from jax.sharding import PartitionSpec as P


def shifted(block, axis, distance):
    devices = range(lax.axis_size(axis))
    route = [(i - distance, i) for i in devices if i - distance in devices]
    return lax.ppermute(block, axis, route)


def general_device(propagator, rising_op, energies, hyb_particle, hyb_hole, sector_sizes):
    t_dev = propagator.shape[1]
    states = propagator.shape[2]
    time_count = t_dev * lax.axis_size("tm")
    step_size = 1.0 / time_count
    positions = jnp.arange(states, dtype=jnp.int32)
    live_mask = positions < sector_sizes[0]
    square = live_mask[:, None] & live_mask[None, :]
    masked_prop = jnp.where(square[None], propagator[0], jnp.zeros((), jnp.bfloat16))
    operator = rising_op[0]
    raised = jnp.einsum(
        "ik,tkl->til", operator, masked_prop, preferred_element_type=jnp.float32
    ).astype(jnp.bfloat16)
    upward = jnp.einsum("tik,jk->tij", raised, operator, preferred_element_type=jnp.float32).astype(
        jnp.bfloat16
    )
    from_below = shifted(upward, "sector", 1)
    from_above = shifted(masked_prop, "sector", -1)
    lowered = jnp.einsum(
        "ki,tkl->til", operator, from_above, preferred_element_type=jnp.float32
    ).astype(jnp.bfloat16)
    downward = jnp.einsum("tik,kl->til", lowered, operator, preferred_element_type=jnp.float32)
    combined = (
        hyb_particle[:, None, None] * from_below.astype(jnp.float32)
        + hyb_hole[:, None, None] * downward
    )
    self_energy = jnp.where(square[None], combined, jnp.zeros((), jnp.float32)).astype(jnp.bfloat16)
    rows_each = states // lax.axis_size("tm")
    first_row = lax.axis_index("tm") * rows_each
    lag_rows = lax.all_to_all(self_energy, "tm", split_axis=1, concat_axis=0, tiled=True)
    history = lax.all_gather(masked_prop, "tm", axis=0, tiled=True)
    mirrored = jnp.concatenate([history[::-1], history], 0)
    slots = jnp.arange(time_count, dtype=jnp.int32)
    wide_slots = jnp.arange(time_count + 1, dtype=jnp.int32)

    def pair_step(lag, sums):
        forward, backward = sums
        other = time_count - 1 - lag
        window = lax.dynamic_slice_in_dim(mirrored, lag, time_count + 1, 0)
        near = lax.dynamic_index_in_dim(lag_rows, lag, 0, keepdims=False)
        far = lax.dynamic_index_in_dim(lag_rows, other, 0, keepdims=False)
        left = jnp.where((wide_slots < time_count - lag)[:, None, None], near[None], far[None])
        product = jnp.einsum("uik,ukl->uil", left, window, preferred_element_type=jnp.float32)
        backward = backward + jnp.where(
            (slots < time_count - lag)[:, None, None],
            product[:time_count],
            jnp.zeros((), jnp.float32),
        )
        forward = forward + jnp.where(
            (slots >= time_count - lag - 1)[:, None, None], product[1:], jnp.zeros((), jnp.float32)
        )
        return (forward, backward)

    empty_rows = jnp.zeros((time_count, rows_each, states), jnp.float32)
    forward, backward = lax.fori_loop(0, time_count // 2, pair_step, (empty_rows, empty_rows))
    convolved = step_size * (forward + backward[::-1])
    row_ids = first_row + jnp.arange(rows_each, dtype=jnp.int32)
    row_rates = lax.dynamic_slice_in_dim(energies[0], first_row, rows_each, 0)
    decay_rows = jnp.exp(-step_size * row_rates)

    def advance(running, term):
        running = decay_rows[:, None] * running + term
        return (running, running)

    _, summed = lax.scan(advance, jnp.zeros((rows_each, states), jnp.float32), convolved)
    moments = jnp.arange(time_count).astype(jnp.float32) * step_size
    live_rows = row_ids < sector_sizes[0]
    free_part = jnp.where(
        live_rows[None, :],
        jnp.exp(-row_rates[None, :] * moments[:, None]),
        jnp.zeros((), jnp.float32),
    )
    diagonal = jnp.where(
        (row_ids[:, None] == positions[None, :])[None],
        free_part[:, :, None],
        jnp.zeros((), jnp.float32),
    )
    new_rows = (diagonal - step_size * summed).astype(jnp.bfloat16)
    return lax.all_to_all(new_rows, "tm", split_axis=0, concat_axis=1, tiled=True)[None]


MESH = pl.DeviceIdType.MESH
ROW_TILE = 16
LANES = 128
SUBLANES = 8
CORE, ACROSS, ALONG = 1, 2, 4
PIECES = 4
VMEM_GRANT = 211 * 2**18


def flipped(index, mask):
    bit = 1
    while bit <= mask:
        if mask & bit:
            index = index + bit - 2 * bit * lax.rem(lax.div(index, bit), 2)
        bit *= 2
    return index


def fused_kernel(
    times,
    sectors,
    size_hbm,
    particle_hbm,
    hole_hbm,
    prop_hbm,
    operator_hbm,
    energy_hbm,
    out_ref,
    size_ref,
    particle_ref,
    hole_ref,
    energy_ref,
    history,
    operator,
    raiser,
    raiser_turned,
    turned,
    turned_in,
    pair,
    up_rows,
    down_rows,
    below,
    above,
    energy_in,
    sums,
    running,
    fresh,
    strengths,
    load_sem,
    turned_send,
    turned_recv,
    up_send,
    up_recv,
    down_send,
    down_recv,
    piece_send,
    piece_recv,
    strength_send,
    strength_recv,
    out_send,
    out_recv,
):
    states = prop_hbm.shape[-1]
    rows = states // times
    quarter = states // PIECES
    step_size = 1.0 / times
    me = lax.axis_index("tm")
    sector = lax.axis_index("sector")
    has_below = sector > 0
    has_above = sector < sectors - 1
    core = lax.rem(me, 2)
    even = me - core
    partner = flipped(me, CORE)
    x_even, y_even = flipped(even, ACROSS), flipped(even, ALONG)
    d_even = flipped(even, ACROSS | ALONG)

    loads = [
        pltpu.make_async_copy(src, dst, load_sem.at[i])
        for i, (src, dst) in enumerate(
            [
                (prop_hbm.at[0, 0], history.at[me]),
                (size_hbm, size_ref),
                (operator_hbm.at[0], operator),
                (particle_hbm, particle_ref),
                (hole_hbm, hole_ref),
                (energy_hbm, energy_ref),
            ]
        )
    ]
    barrier = pltpu.get_barrier_semaphore()
    for mask in range(1, times):
        pl.semaphore_signal(
            barrier, inc=1, device_id={"tm": flipped(me, mask)}, device_id_type=MESH
        )

    @pl.when(has_below)
    def _():
        pl.semaphore_signal(barrier, inc=1, device_id={"sector": sector - 1}, device_id_type=MESH)

    @pl.when(has_above)
    def _():
        pl.semaphore_signal(barrier, inc=1, device_id={"sector": sector + 1}, device_id_type=MESH)

    for load in loads:
        load.start()

    def row_block(index):
        return pl.ds(pl.multiple_of(index * rows, rows), rows)

    def piece_copy(step, time, q, kind):
        piece = history.at[time, pl.ds(pl.multiple_of(q * quarter, quarter), quarter)]
        return pltpu.make_async_remote_copy(
            src_ref=piece,
            dst_ref=piece,
            send_sem=piece_send,
            recv_sem=piece_recv.at[time, kind],
            device_id={"tm": flipped(me, step)},
            device_id_type=MESH,
        )

    mine = [2 * core, 2 * core + 1]
    other = [2 - 2 * core, 3 - 2 * core]

    def turned_copy(step=1):
        return pltpu.make_async_remote_copy(
            src_ref=turned,
            dst_ref=turned_in,
            send_sem=turned_send,
            recv_sem=turned_recv,
            device_id={"sector": sector + step},
            device_id_type=MESH,
        )

    def signal_of(slot):
        return slot // 2 if slot < times - 2 else slot - times // 2 + 1

    def up_copy(slot, time, step=1):
        block = row_block(time)
        return pltpu.make_async_remote_copy(
            src_ref=up_rows.at[block],
            dst_ref=below.at[block],
            send_sem=up_send,
            recv_sem=up_recv.at[signal_of(slot)],
            device_id={"sector": sector + step},
            device_id_type=MESH,
        )

    def down_copy(slot, time, step=-1):
        block = row_block(time)
        return pltpu.make_async_remote_copy(
            src_ref=down_rows.at[block],
            dst_ref=above.at[block],
            send_sem=down_send,
            recv_sem=down_recv.at[signal_of(slot)],
            device_id={"sector": sector + step},
            device_id_type=MESH,
        )

    def strength_copy(mask, block, count=1):
        return pltpu.make_async_remote_copy(
            src_ref=strengths.at[pl.ds(block, count)],
            dst_ref=strengths.at[pl.ds(block, count)],
            send_sem=strength_send,
            recv_sem=strength_recv,
            device_id={"tm": flipped(me, mask)},
            device_id_type=MESH,
        )

    def out_copy(moment, place):
        return pltpu.make_async_remote_copy(
            src_ref=fresh.at[moment],
            dst_ref=out_ref.at[0, 0, row_block(place)],
            send_sem=out_send,
            recv_sem=out_recv,
            device_id={"tm": moment},
            device_id_type=MESH,
        )

    loads[0].wait()
    for load in loads[3:]:
        load.wait()
    first_line = lax.broadcasted_iota(jnp.int32, strengths.shape[1:], 0) == 0
    strengths[me] = jnp.where(first_line, particle_ref[0], hole_ref[0])
    neighbours = jnp.where(has_below, 1, 0) + jnp.where(has_above, 1, 0)
    pl.semaphore_wait(barrier, times - 1 + neighbours)

    def links_start(time):
        for step, r in ((ACROSS, 0), (ALONG, 1), (ACROSS, 1), (ALONG, 0)):
            piece_copy(step, time, mine[r], r).start()

    def share_start(time):
        for q in mine:
            piece_copy(CORE, time, q, 2).start()

    for mask in range(1, times):
        strength_copy(mask, me).start()
    for r, q in enumerate(other):
        piece_copy(CORE, me, q, r).start()

    @pl.when(core == 0)
    def _():
        links_start(me)

    share_start(me)
    loads[2].wait()
    row_ids = me * rows + lax.broadcasted_iota(jnp.int32, (rows, states), 0)
    column_ids = lax.broadcasted_iota(jnp.int32, (rows, states), 1)
    on_diagonal = row_ids == column_ids
    chosen = jnp.where(on_diagonal, 1.0, 0.0).astype(jnp.bfloat16)
    turned[...] = lax.dot_general(
        chosen, operator[...], (((1,), (1,)), ((), ())), preferred_element_type=jnp.float32
    ).astype(jnp.bfloat16)

    @pl.when(has_above)
    def _():
        turned_copy().start()

    loads[1].wait()
    size = size_ref[0]
    live_columns = lax.broadcasted_iota(jnp.int32, (states, states), 1) < size
    live_line = column_ids < size
    raiser[...] = jnp.where(live_columns, operator[...].astype(jnp.float32), 0.0).astype(
        jnp.bfloat16
    )
    for r, q in enumerate(mine):
        piece_copy(CORE, partner, q, r).wait_recv()

    links_start(partner)

    @pl.when(core == 1)
    def _():
        links_start(me)

    def product_of(left, time):
        return jnp.dot(left, history[time], preferred_element_type=jnp.float32)

    def send_up(slot, time, raised):
        up_rows[row_block(time)] = jnp.dot(
            raised.astype(jnp.bfloat16), raiser_turned[...], preferred_element_type=jnp.float32
        ).astype(jnp.bfloat16)

        @pl.when(has_above)
        def _():
            up_copy(slot, time).start()

    def send_down(slot, time, lowered):
        down_rows[row_block(time)] = jnp.where(live_line, lowered, 0.0).astype(jnp.bfloat16)

        @pl.when(has_below)
        def _():
            down_copy(slot, time).start()

    def arrive(step, time, r):
        piece_copy(step, time, mine[r], r).wait_recv()
        piece_copy(CORE, time, mine[r], 2).start()

    def relay(step, time, r):
        piece_copy(step, time, mine[r], r).start()

    def shared(time):
        rest = history.at[time, pl.ds(0, states // 2)]
        pltpu.make_async_remote_copy(
            src_ref=rest,
            dst_ref=rest,
            send_sem=piece_send,
            recv_sem=piece_recv.at[time, 2],
            device_id={"tm": partner},
            device_id_type=MESH,
        ).wait_recv()

    order = [me, partner, x_even, y_even, x_even + 1, y_even + 1, d_even, d_even + 1]
    last = order[-1]

    pair[0:rows] = raiser[row_block(me)]
    raiser_turned[...] = raiser[...].T
    send_up(0, me, product_of(pair[0:rows], me))
    shared(partner)
    send_up(1, partner, product_of(pair[0:rows], partner))

    rates = jnp.sum(
        jnp.where(on_diagonal, energy_ref[...], jnp.zeros((), jnp.float32)), axis=1, keepdims=True
    )
    decay = jnp.exp(-step_size * rates)
    running[...] = jnp.zeros_like(running)
    sums[...] = jnp.zeros_like(sums)

    @pl.when(jnp.logical_not(has_below))
    def _():
        turned_in[...] = jnp.zeros_like(turned_in)
        below[...] = jnp.zeros_like(below)

    @pl.when(jnp.logical_not(has_above))
    def _():
        above[...] = jnp.zeros_like(above)

    arrive(ACROSS, x_even, 0)
    relay(ALONG, x_even, 0)
    arrive(ALONG, y_even, 1)
    relay(ACROSS, y_even, 1)

    @pl.when(has_below)
    def _():
        turned_copy(-1).wait_recv()

    pair[rows : 2 * rows] = jnp.where(
        live_line, turned_in[...].astype(jnp.float32), 0.0
    ).astype(jnp.bfloat16)
    for slot in range(2):
        send_down(slot, order[slot], product_of(pair[rows : 2 * rows], order[slot]))

    arrive(ACROSS, x_even, 1)
    arrive(ALONG, y_even, 0)

    def both(slot):
        time = order[slot]
        shared(time)
        result = product_of(pair[...], time)
        send_down(slot, time, result[rows : 2 * rows])
        send_up(slot, time, result[0:rows])

    live_rows = (row_ids < size) & (column_ids < size)
    shown = on_diagonal & (row_ids < size)

    def wait_rows(buffer, send, recv, slots, step):
        block = buffer.at[pl.ds(0, len(slots) * rows)]
        pltpu.make_async_remote_copy(
            src_ref=block,
            dst_ref=block,
            send_sem=send,
            recv_sem=recv.at[signal_of(slots[0])],
            device_id={"sector": sector + step},
            device_id_type=MESH,
        ).wait_recv()

    def combine(*slots):
        places = [row_block(order[slot]) for slot in slots]

        @pl.when(has_below)
        def _():
            wait_rows(below, up_send, up_recv, slots, -1)

        @pl.when(has_above)
        def _():
            wait_rows(above, down_send, down_recv, slots, 1)

        lowered = jnp.concatenate([above[place] for place in places], 0)
        downward = jnp.dot(lowered, operator[...], preferred_element_type=jnp.float32)
        for i, (slot, place) in enumerate(zip(slots, places)):
            level = strengths[order[slot]]
            combined = (
                level[0:1, 0:1] * below[place].astype(jnp.float32)
                + level[1:2, 0:1] * downward[i * rows : (i + 1) * rows]
            )
            energy_in[place] = jnp.where(live_rows, combined, jnp.zeros((), jnp.float32)).astype(
                jnp.bfloat16
            )

    def accumulate(lag_even, *bases):
        left = energy_in[pl.ds(pl.multiple_of(lag_even * rows, rows), 2 * rows)]
        for base in bases:
            first = pl.multiple_of((lag_even + base) * rows, rows)
            sums[pl.ds(first, 2 * rows)] += jnp.dot(
                left, history[base], preferred_element_type=jnp.float32
            )

    def convolve(lag_even, *bases):
        @pl.when(lag_even + bases[0] < times)
        def _():
            accumulate(lag_even, *bases)

    def finish(moment):
        place = row_block(moment)
        value = decay * running[...] + step_size * sums[place]
        running[...] = value
        instant = jnp.asarray(moment, jnp.int32).astype(jnp.float32) * step_size
        free_part = jnp.where(shown, jnp.exp(-rates * instant), jnp.zeros((), jnp.float32))
        fresh[moment] = jnp.where(
            live_rows, free_part - step_size * value, jnp.zeros((), jnp.float32)
        ).astype(jnp.bfloat16)

        @pl.when((me != moment))
        def _():
            out_copy(moment, me).start()

        @pl.when(me == moment)
        def _():
            out_ref[0, 0, row_block(me)] = fresh[moment]

    x_odd, y_odd = x_even + 1, y_even + 1
    strength_copy(CORE, 0, times - 1).wait_recv()
    both(2)
    both(3)
    combine(0, 1)
    convolve(even, even, even + 1)
    arrive(ACROSS, x_odd, 0)
    relay(ALONG, x_odd, 0)
    arrive(ALONG, y_odd, 1)
    relay(ACROSS, y_odd, 1)
    convolve(even, x_even)
    convolve(even, y_even)
    arrive(ACROSS, x_odd, 1)
    arrive(ALONG, y_odd, 0)
    combine(2, 3)
    both(4)
    both(5)
    arrive(ALONG, d_even, 0)
    arrive(ACROSS, d_even, 1)
    convolve(even, x_odd)
    convolve(even, y_odd)
    both(6)
    accumulate(even, d_even)
    arrive(ALONG, last, 0)
    arrive(ACROSS, last, 1)
    combine(4, 5)

    def finish_between(start, stop, allowed):
        for moment in range(start, stop, 2):

            @pl.when(allowed & (moment < d_even))
            def _():
                finish(moment)
                finish(moment + 1)

    first_half = d_even >= times // 2
    convolve(x_even, even, even + 1)
    convolve(x_even, x_even, x_odd)
    finish_between(0, times // 2, first_half)
    convolve(y_even, y_even, y_odd)
    finish_between(0, times // 2, jnp.logical_not(first_half))
    both(7)
    accumulate(x_even, y_even, y_odd)
    accumulate(y_even, x_even, x_odd)
    convolve(y_even, even, even + 1)
    finish_between(times // 2, times, first_half)
    accumulate(even, last)
    convolve(x_even, d_even, last)
    convolve(y_even, d_even, last)
    combine(6)
    sums[row_block(d_even)] += jnp.dot(
        energy_in[row_block(d_even)], history[0], preferred_element_type=jnp.float32
    )
    finish(d_even)
    combine(7)
    for moment in range(0, times, 2):

        @pl.when(d_even + moment < times)
        def _():
            accumulate(d_even, moment, moment + 1)
            if moment > 0:
                finish(d_even + moment)
            finish(d_even + moment + 1)

    strength_copy(CORE, 0, times - 1).wait_send()
    blocks = history.at[pl.ds(0, times - 1)]
    pltpu.make_async_remote_copy(
        src_ref=blocks,
        dst_ref=blocks,
        send_sem=piece_send,
        recv_sem=piece_recv.at[0, 0],
        device_id={"tm": partner},
        device_id_type=MESH,
    ).wait_send()

    def wait_sent(buffer, send, recv, step):
        pltpu.make_async_remote_copy(
            src_ref=buffer,
            dst_ref=buffer,
            send_sem=send,
            recv_sem=recv.at[0],
            device_id={"sector": sector + step},
            device_id_type=MESH,
        ).wait_send()

    @pl.when(has_below)
    def _():
        wait_sent(down_rows, down_send, down_recv, -1)

    @pl.when(has_above)
    def _():
        turned_copy().wait_send()
        wait_sent(up_rows, up_send, up_recv, 1)

    results = fresh.at[pl.ds(0, times - 1)]
    leaving = pltpu.make_async_remote_copy(
        src_ref=results,
        dst_ref=results,
        send_sem=out_send,
        recv_sem=out_recv,
        device_id={"tm": partner},
        device_id_type=MESH,
    )
    leaving.wait_recv()
    leaving.wait_send()


def fused_device(propagator, rising_op, energies, hyb_particle, hyb_hole, sector_sizes):
    times = lax.axis_size("tm")
    states = propagator.shape[-1]
    rows = states // times
    square = (states, states)
    narrow, wide = jnp.bfloat16, jnp.float32
    anywhere = pl.BlockSpec(memory_space=pltpu.HBM)
    dma = pltpu.SemaphoreType.DMA
    return pl.pallas_call(
        functools.partial(fused_kernel, times, lax.axis_size("sector")),
        out_shape=jax.ShapeDtypeStruct(propagator.shape, narrow),
        in_specs=[anywhere] * 6,
        out_specs=pl.BlockSpec(memory_space=pltpu.VMEM),
        scratch_shapes=[
            pltpu.SMEM((1,), jnp.int32),
            pltpu.SMEM((1,), wide),
            pltpu.SMEM((1,), wide),
            pltpu.VMEM(energies.shape, wide),
            pltpu.VMEM((times,) + square, narrow),
            pltpu.VMEM(square, narrow),
            pltpu.VMEM(square, narrow),
            pltpu.VMEM(square, narrow),
            pltpu.VMEM((rows, states), narrow),
            pltpu.VMEM((rows, states), narrow),
            pltpu.VMEM((2 * rows, states), narrow),
            pltpu.VMEM(square, narrow),
            pltpu.VMEM(square, narrow),
            pltpu.VMEM(square, narrow),
            pltpu.VMEM(square, narrow),
            pltpu.VMEM(square, narrow),
            pltpu.VMEM((states + rows, states), wide),
            pltpu.VMEM((rows, states), wide),
            pltpu.VMEM((times, rows, states), narrow),
            pltpu.VMEM((times, SUBLANES, LANES), wide),
            dma((6,)),
            dma,
            dma,
            dma,
            dma((times // 2 + 1,)),
            dma,
            dma((times // 2 + 1,)),
            dma,
            dma((times, 3)),
            dma,
            dma,
            dma,
            dma,
        ],
        compiler_params=pltpu.CompilerParams(
            collective_id=0, has_side_effects=True, vmem_limit_bytes=VMEM_GRANT
        ),
    )(sector_sizes, hyb_particle, hyb_hole, propagator, rising_op, energies)


def per_device(propagator, rising_op, energies, hyb_particle, hyb_hole, sector_sizes):
    times = lax.axis_size("tm")
    states = propagator.shape[-1]
    fits = (
        propagator.shape[1] == 1
        and times == (CORE | ACROSS | ALONG) + 1
        and states % (times * ROW_TILE) == 0
        and states % (PIECES * ROW_TILE) == 0
        and states % LANES == 0
    )
    chosen = fused_device if fits else general_device
    return chosen(propagator, rising_op, energies, hyb_particle, hyb_hole, sector_sizes)


def solution(mesh):
    placed = (
        P("sector", "tm", None, None),
        P("sector", None, None),
        P("sector", None),
        P("tm"),
        P("tm"),
        P("sector"),
    )
    return jax.shard_map(
        per_device,
        mesh=mesh,
        in_specs=placed,
        out_specs=P("sector", "tm", None, None),
        check_vma=False,
    )
```

```python
import functools
import jax
import jax.numpy as jnp
from jax import lax
from jax.experimental import pallas as pl
from jax.experimental.pallas import tpu as pltpu
from jax.sharding import PartitionSpec as P


def shifted(block, axis, distance):
    devices = range(lax.axis_size(axis))
    route = [(i - distance, i) for i in devices if i - distance in devices]
    return lax.ppermute(block, axis, route)


def general_device(propagator, rising_op, energies, hyb_particle, hyb_hole, sector_sizes):
    t_dev = propagator.shape[1]
    states = propagator.shape[2]
    time_count = t_dev * lax.axis_size("tm")
    step_size = 1.0 / time_count
    positions = jnp.arange(states, dtype=jnp.int32)
    live_mask = positions < sector_sizes[0]
    square = live_mask[:, None] & live_mask[None, :]
    masked_prop = jnp.where(square[None], propagator[0], jnp.zeros((), jnp.bfloat16))
    operator = rising_op[0]
    raised = jnp.einsum(
        "ik,tkl->til", operator, masked_prop, preferred_element_type=jnp.float32
    ).astype(jnp.bfloat16)
    upward = jnp.einsum("tik,jk->tij", raised, operator, preferred_element_type=jnp.float32).astype(
        jnp.bfloat16
    )
    from_below = shifted(upward, "sector", 1)
    from_above = shifted(masked_prop, "sector", -1)
    lowered = jnp.einsum(
        "ki,tkl->til", operator, from_above, preferred_element_type=jnp.float32
    ).astype(jnp.bfloat16)
    downward = jnp.einsum("tik,kl->til", lowered, operator, preferred_element_type=jnp.float32)
    combined = (
        hyb_particle[:, None, None] * from_below.astype(jnp.float32)
        + hyb_hole[:, None, None] * downward
    )
    self_energy = jnp.where(square[None], combined, jnp.zeros((), jnp.float32)).astype(jnp.bfloat16)
    rows_each = states // lax.axis_size("tm")
    first_row = lax.axis_index("tm") * rows_each
    lag_rows = lax.all_to_all(self_energy, "tm", split_axis=1, concat_axis=0, tiled=True)
    history = lax.all_gather(masked_prop, "tm", axis=0, tiled=True)
    mirrored = jnp.concatenate([history[::-1], history], 0)
    slots = jnp.arange(time_count, dtype=jnp.int32)
    wide_slots = jnp.arange(time_count + 1, dtype=jnp.int32)

    def pair_step(lag, sums):
        forward, backward = sums
        other = time_count - 1 - lag
        window = lax.dynamic_slice_in_dim(mirrored, lag, time_count + 1, 0)
        near = lax.dynamic_index_in_dim(lag_rows, lag, 0, keepdims=False)
        far = lax.dynamic_index_in_dim(lag_rows, other, 0, keepdims=False)
        left = jnp.where((wide_slots < time_count - lag)[:, None, None], near[None], far[None])
        product = jnp.einsum("uik,ukl->uil", left, window, preferred_element_type=jnp.float32)
        backward = backward + jnp.where(
            (slots < time_count - lag)[:, None, None],
            product[:time_count],
            jnp.zeros((), jnp.float32),
        )
        forward = forward + jnp.where(
            (slots >= time_count - lag - 1)[:, None, None], product[1:], jnp.zeros((), jnp.float32)
        )
        return (forward, backward)

    empty_rows = jnp.zeros((time_count, rows_each, states), jnp.float32)
    forward, backward = lax.fori_loop(0, time_count // 2, pair_step, (empty_rows, empty_rows))
    convolved = step_size * (forward + backward[::-1])
    row_ids = first_row + jnp.arange(rows_each, dtype=jnp.int32)
    row_rates = lax.dynamic_slice_in_dim(energies[0], first_row, rows_each, 0)
    decay_rows = jnp.exp(-step_size * row_rates)

    def advance(running, term):
        running = decay_rows[:, None] * running + term
        return (running, running)

    _, summed = lax.scan(advance, jnp.zeros((rows_each, states), jnp.float32), convolved)
    moments = jnp.arange(time_count).astype(jnp.float32) * step_size
    live_rows = row_ids < sector_sizes[0]
    free_part = jnp.where(
        live_rows[None, :],
        jnp.exp(-row_rates[None, :] * moments[:, None]),
        jnp.zeros((), jnp.float32),
    )
    diagonal = jnp.where(
        (row_ids[:, None] == positions[None, :])[None],
        free_part[:, :, None],
        jnp.zeros((), jnp.float32),
    )
    new_rows = (diagonal - step_size * summed).astype(jnp.bfloat16)
    return lax.all_to_all(new_rows, "tm", split_axis=0, concat_axis=1, tiled=True)[None]


MESH = pl.DeviceIdType.MESH
ROW_TILE = 16
LANES = 128
SUBLANES = 8
CORE, ACROSS, ALONG = 1, 2, 4
PIECES = 4
VMEM_GRANT = 211 * 2**18


def flipped(index, mask):
    bit = 1
    while bit <= mask:
        if mask & bit:
            index = index + bit - 2 * bit * lax.rem(lax.div(index, bit), 2)
        bit *= 2
    return index


def fused_kernel(
    times,
    sectors,
    size_hbm,
    particle_hbm,
    hole_hbm,
    prop_hbm,
    operator_hbm,
    energy_hbm,
    out_ref,
    size_ref,
    particle_ref,
    hole_ref,
    energy_ref,
    history,
    operator,
    raiser,
    raiser_turned,
    turned,
    turned_in,
    pair,
    up_rows,
    down_rows,
    below,
    above,
    energy_in,
    sums,
    running,
    fresh,
    strengths,
    load_sem,
    turned_send,
    turned_recv,
    up_send,
    up_recv,
    down_send,
    down_recv,
    piece_send,
    piece_recv,
    strength_send,
    strength_recv,
    out_send,
    out_recv,
):
    states = prop_hbm.shape[-1]
    rows = states // times
    quarter = states // PIECES
    step_size = 1.0 / times
    me = lax.axis_index("tm")
    sector = lax.axis_index("sector")
    has_below = sector > 0
    has_above = sector < sectors - 1
    core = lax.rem(me, 2)
    even = me - core
    partner = flipped(me, CORE)
    x_even, y_even = flipped(even, ACROSS), flipped(even, ALONG)
    d_even = flipped(even, ACROSS | ALONG)

    loads = [
        pltpu.make_async_copy(src, dst, load_sem.at[i])
        for i, (src, dst) in enumerate(
            [
                (prop_hbm.at[0, 0], history.at[me]),
                (size_hbm, size_ref),
                (operator_hbm.at[0], operator),
                (particle_hbm, particle_ref),
                (hole_hbm, hole_ref),
                (energy_hbm, energy_ref),
            ]
        )
    ]
    barrier = pltpu.get_barrier_semaphore()
    for mask in range(1, times):
        pl.semaphore_signal(
            barrier, inc=1, device_id={"tm": flipped(me, mask)}, device_id_type=MESH
        )

    @pl.when(has_below)
    def _():
        pl.semaphore_signal(barrier, inc=1, device_id={"sector": sector - 1}, device_id_type=MESH)

    @pl.when(has_above)
    def _():
        pl.semaphore_signal(barrier, inc=1, device_id={"sector": sector + 1}, device_id_type=MESH)

    for load in loads:
        load.start()

    def row_block(index):
        return pl.ds(pl.multiple_of(index * rows, rows), rows)

    def piece_copy(step, time, q, kind):
        piece = history.at[time, pl.ds(pl.multiple_of(q * quarter, quarter), quarter)]
        return pltpu.make_async_remote_copy(
            src_ref=piece,
            dst_ref=piece,
            send_sem=piece_send,
            recv_sem=piece_recv.at[time, kind],
            device_id={"tm": flipped(me, step)},
            device_id_type=MESH,
        )

    mine = [2 * core, 2 * core + 1]
    other = [2 - 2 * core, 3 - 2 * core]

    def turned_copy(step=1):
        return pltpu.make_async_remote_copy(
            src_ref=turned,
            dst_ref=turned_in,
            send_sem=turned_send,
            recv_sem=turned_recv,
            device_id={"sector": sector + step},
            device_id_type=MESH,
        )

    def signal_of(slot):
        return slot // 2 if slot < times - 2 else slot - times // 2 + 1

    def up_copy(slot, time, step=1):
        block = row_block(time)
        return pltpu.make_async_remote_copy(
            src_ref=up_rows.at[block],
            dst_ref=below.at[block],
            send_sem=up_send,
            recv_sem=up_recv.at[signal_of(slot)],
            device_id={"sector": sector + step},
            device_id_type=MESH,
        )

    def down_copy(slot, time, step=-1):
        block = row_block(time)
        return pltpu.make_async_remote_copy(
            src_ref=down_rows.at[block],
            dst_ref=above.at[block],
            send_sem=down_send,
            recv_sem=down_recv.at[signal_of(slot)],
            device_id={"sector": sector + step},
            device_id_type=MESH,
        )

    def strength_copy(mask, block, count=1):
        return pltpu.make_async_remote_copy(
            src_ref=strengths.at[pl.ds(block, count)],
            dst_ref=strengths.at[pl.ds(block, count)],
            send_sem=strength_send,
            recv_sem=strength_recv,
            device_id={"tm": flipped(me, mask)},
            device_id_type=MESH,
        )

    def out_copy(moment, place):
        return pltpu.make_async_remote_copy(
            src_ref=fresh.at[moment],
            dst_ref=out_ref.at[0, 0, row_block(place)],
            send_sem=out_send,
            recv_sem=out_recv,
            device_id={"tm": moment},
            device_id_type=MESH,
        )

    loads[0].wait()
    for load in loads[3:]:
        load.wait()
    first_line = lax.broadcasted_iota(jnp.int32, strengths.shape[1:], 0) == 0
    strengths[me] = jnp.where(first_line, particle_ref[0], hole_ref[0])
    neighbours = jnp.where(has_below, 1, 0) + jnp.where(has_above, 1, 0)
    pl.semaphore_wait(barrier, times - 1 + neighbours)

    def links_start(time):
        for step, r in ((ACROSS, 0), (ALONG, 1), (ACROSS, 1), (ALONG, 0)):
            piece_copy(step, time, mine[r], r).start()

    def share_start(time):
        for q in mine:
            piece_copy(CORE, time, q, 2).start()

    for mask in range(1, times):
        strength_copy(mask, me).start()
    for r, q in enumerate(other):
        piece_copy(CORE, me, q, r).start()

    @pl.when(core == 0)
    def _():
        links_start(me)

    share_start(me)
    loads[2].wait()
    row_ids = me * rows + lax.broadcasted_iota(jnp.int32, (rows, states), 0)
    column_ids = lax.broadcasted_iota(jnp.int32, (rows, states), 1)
    on_diagonal = row_ids == column_ids
    chosen = jnp.where(on_diagonal, 1.0, 0.0).astype(jnp.bfloat16)
    turned[...] = lax.dot_general(
        chosen, operator[...], (((1,), (1,)), ((), ())), preferred_element_type=jnp.float32
    ).astype(jnp.bfloat16)

    @pl.when(has_above)
    def _():
        turned_copy().start()

    loads[1].wait()
    size = size_ref[0]
    live_columns = lax.broadcasted_iota(jnp.int32, (states, states), 1) < size
    live_line = column_ids < size
    raiser[...] = jnp.where(live_columns, operator[...].astype(jnp.float32), 0.0).astype(
        jnp.bfloat16
    )
    for r, q in enumerate(mine):
        piece_copy(CORE, partner, q, r).wait_recv()

    links_start(partner)

    @pl.when(core == 1)
    def _():
        links_start(me)

    def product_of(left, time):
        return jnp.dot(left, history[time], preferred_element_type=jnp.float32)

    def send_up(slot, time, raised):
        up_rows[row_block(time)] = jnp.dot(
            raised.astype(jnp.bfloat16), raiser_turned[...], preferred_element_type=jnp.float32
        ).astype(jnp.bfloat16)

        @pl.when(has_above)
        def _():
            up_copy(slot, time).start()

    def send_down(slot, time, lowered):
        down_rows[row_block(time)] = jnp.where(live_line, lowered, 0.0).astype(jnp.bfloat16)

        @pl.when(has_below)
        def _():
            down_copy(slot, time).start()

    def arrive(step, time, r):
        piece_copy(step, time, mine[r], r).wait_recv()
        piece_copy(CORE, time, mine[r], 2).start()

    def relay(step, time, r):
        piece_copy(step, time, mine[r], r).start()

    def shared(time):
        rest = history.at[time, pl.ds(0, states // 2)]
        pltpu.make_async_remote_copy(
            src_ref=rest,
            dst_ref=rest,
            send_sem=piece_send,
            recv_sem=piece_recv.at[time, 2],
            device_id={"tm": partner},
            device_id_type=MESH,
        ).wait_recv()

    order = [me, partner, x_even, y_even, x_even + 1, y_even + 1, d_even, d_even + 1]
    last = order[-1]

    pair[0:rows] = raiser[row_block(me)]
    raiser_turned[...] = raiser[...].T
    send_up(0, me, product_of(pair[0:rows], me))
    shared(partner)
    send_up(1, partner, product_of(pair[0:rows], partner))

    rates = jnp.sum(
        jnp.where(on_diagonal, energy_ref[...], jnp.zeros((), jnp.float32)), axis=1, keepdims=True
    )
    decay = jnp.exp(-step_size * rates)
    running[...] = jnp.zeros_like(running)
    sums[...] = jnp.zeros_like(sums)

    @pl.when(jnp.logical_not(has_below))
    def _():
        turned_in[...] = jnp.zeros_like(turned_in)
        below[...] = jnp.zeros_like(below)

    @pl.when(jnp.logical_not(has_above))
    def _():
        above[...] = jnp.zeros_like(above)

    arrive(ACROSS, x_even, 0)
    relay(ALONG, x_even, 0)
    arrive(ALONG, y_even, 1)
    relay(ACROSS, y_even, 1)

    @pl.when(has_below)
    def _():
        turned_copy(-1).wait_recv()

    pair[rows : 2 * rows] = jnp.where(
        live_line, turned_in[...].astype(jnp.float32), 0.0
    ).astype(jnp.bfloat16)
    for slot in range(2):
        send_down(slot, order[slot], product_of(pair[rows : 2 * rows], order[slot]))

    arrive(ACROSS, x_even, 1)
    arrive(ALONG, y_even, 0)

    def both(slot):
        time = order[slot]
        shared(time)
        result = product_of(pair[...], time)
        send_down(slot, time, result[rows : 2 * rows])
        send_up(slot, time, result[0:rows])

    live_rows = (row_ids < size) & (column_ids < size)
    shown = on_diagonal & (row_ids < size)

    def wait_rows(buffer, send, recv, slots, step):
        block = buffer.at[pl.ds(0, len(slots) * rows)]
        pltpu.make_async_remote_copy(
            src_ref=block,
            dst_ref=block,
            send_sem=send,
            recv_sem=recv.at[signal_of(slots[0])],
            device_id={"sector": sector + step},
            device_id_type=MESH,
        ).wait_recv()

    def combine(*slots):
        places = [row_block(order[slot]) for slot in slots]

        @pl.when(has_below)
        def _():
            wait_rows(below, up_send, up_recv, slots, -1)

        @pl.when(has_above)
        def _():
            wait_rows(above, down_send, down_recv, slots, 1)

        lowered = jnp.concatenate([above[place] for place in places], 0)
        downward = jnp.dot(lowered, operator[...], preferred_element_type=jnp.float32)
        for i, (slot, place) in enumerate(zip(slots, places)):
            level = strengths[order[slot]]
            combined = (
                level[0:1, 0:1] * below[place].astype(jnp.float32)
                + level[1:2, 0:1] * downward[i * rows : (i + 1) * rows]
            )
            energy_in[place] = jnp.where(live_rows, combined, jnp.zeros((), jnp.float32)).astype(
                jnp.bfloat16
            )

    def accumulate(lag_even, *bases):
        left = energy_in[pl.ds(pl.multiple_of(lag_even * rows, rows), 2 * rows)]
        for base in bases:
            first = pl.multiple_of((lag_even + base) * rows, rows)
            sums[pl.ds(first, 2 * rows)] += jnp.dot(
                left, history[base], preferred_element_type=jnp.float32
            )

    def convolve(lag_even, *bases):
        @pl.when(lag_even + bases[0] < times)
        def _():
            accumulate(lag_even, *bases)

    def finish(moment):
        place = row_block(moment)
        value = decay * running[...] + step_size * sums[place]
        running[...] = value
        instant = jnp.asarray(moment, jnp.int32).astype(jnp.float32) * step_size
        free_part = jnp.where(shown, jnp.exp(-rates * instant), jnp.zeros((), jnp.float32))
        fresh[moment] = jnp.where(
            live_rows, free_part - step_size * value, jnp.zeros((), jnp.float32)
        ).astype(jnp.bfloat16)

        @pl.when((me != moment))
        def _():
            out_copy(moment, me).start()

        @pl.when(me == moment)
        def _():
            out_ref[0, 0, row_block(me)] = fresh[moment]

    x_odd, y_odd = x_even + 1, y_even + 1
    strength_copy(CORE, 0, times - 1).wait_recv()
    both(2)
    both(3)
    combine(0, 1)
    convolve(even, even, even + 1)
    arrive(ACROSS, x_odd, 0)
    relay(ALONG, x_odd, 0)
    arrive(ALONG, y_odd, 1)
    relay(ACROSS, y_odd, 1)
    convolve(even, x_even)
    convolve(even, y_even)
    arrive(ACROSS, x_odd, 1)
    arrive(ALONG, y_odd, 0)
    combine(2, 3)
    both(4)
    both(5)
    arrive(ALONG, d_even, 0)
    arrive(ACROSS, d_even, 1)
    convolve(even, x_odd)
    convolve(even, y_odd)

    both(6)
    accumulate(even, d_even)

    @pl.when(even == 0)
    def _():
        sums[row_block(x_even)] += jnp.dot(
            energy_in[row_block(x_even)], history[0], preferred_element_type=jnp.float32
        )
        for moment in range(times // 4 + 1):
            finish(moment)

    arrive(ALONG, last, 0)
    arrive(ACROSS, last, 1)
    combine(4, 5)

    def finish_between(start, stop, allowed):
        for moment in range(start, stop, 2):

            @pl.when(allowed & (moment < d_even) & ((even != 0) | (moment > times // 4)))
            def _():
                finish(moment)

            @pl.when(allowed & (moment < d_even) & ((even != 0) | (moment + 1 > times // 4)))
            def _():
                finish(moment + 1)

    first_half = d_even >= times // 2

    def early(allowed):
        @pl.when(allowed)
        def _():
            convolve(x_even, even, even + 1)
            convolve(x_even, x_even, x_odd)
            finish_between(0, times // 2, first_half)
            convolve(y_even, y_even, y_odd)
            finish_between(0, times // 2, jnp.logical_not(first_half))

    early(even == 0)
    both(7)
    early(even != 0)
    convolve(x_even, d_even, last)
    convolve(y_even, d_even, last)

    def finish_next(allowed):
        @pl.when(allowed)
        def _():
            combine(6)
            sums[row_block(d_even)] += jnp.dot(
                energy_in[row_block(d_even)], history[0], preferred_element_type=jnp.float32
            )
            finish(d_even)

    finish_next(even != 0)
    accumulate(x_even, y_even, y_odd)
    accumulate(y_even, x_even, x_odd)
    convolve(y_even, even, even + 1)
    finish_between(times // 2, times, first_half)
    accumulate(even, last)
    finish_next(even == 0)
    combine(7)
    for moment in range(0, times, 2):

        @pl.when(d_even + moment < times)
        def _():
            accumulate(d_even, moment, moment + 1)
            if moment > 0:
                finish(d_even + moment)
            finish(d_even + moment + 1)

    strength_copy(CORE, 0, times - 1).wait_send()
    blocks = history.at[pl.ds(0, times - 1)]
    pltpu.make_async_remote_copy(
        src_ref=blocks,
        dst_ref=blocks,
        send_sem=piece_send,
        recv_sem=piece_recv.at[0, 0],
        device_id={"tm": partner},
        device_id_type=MESH,
    ).wait_send()

    def wait_sent(buffer, send, recv, step):
        pltpu.make_async_remote_copy(
            src_ref=buffer,
            dst_ref=buffer,
            send_sem=send,
            recv_sem=recv.at[0],
            device_id={"sector": sector + step},
            device_id_type=MESH,
        ).wait_send()

    @pl.when(has_below)
    def _():
        wait_sent(down_rows, down_send, down_recv, -1)

    @pl.when(has_above)
    def _():
        turned_copy().wait_send()
        wait_sent(up_rows, up_send, up_recv, 1)

    results = fresh.at[pl.ds(0, times - 1)]
    leaving = pltpu.make_async_remote_copy(
        src_ref=results,
        dst_ref=results,
        send_sem=out_send,
        recv_sem=out_recv,
        device_id={"tm": partner},
        device_id_type=MESH,
    )
    leaving.wait_recv()
    leaving.wait_send()


def fused_device(propagator, rising_op, energies, hyb_particle, hyb_hole, sector_sizes):
    times = lax.axis_size("tm")
    states = propagator.shape[-1]
    rows = states // times
    square = (states, states)
    narrow, wide = jnp.bfloat16, jnp.float32
    anywhere = pl.BlockSpec(memory_space=pltpu.HBM)
    dma = pltpu.SemaphoreType.DMA
    return pl.pallas_call(
        functools.partial(fused_kernel, times, lax.axis_size("sector")),
        out_shape=jax.ShapeDtypeStruct(propagator.shape, narrow),
        in_specs=[anywhere] * 6,
        out_specs=pl.BlockSpec(memory_space=pltpu.VMEM),
        scratch_shapes=[
            pltpu.SMEM((1,), jnp.int32),
            pltpu.SMEM((1,), wide),
            pltpu.SMEM((1,), wide),
            pltpu.VMEM(energies.shape, wide),
            pltpu.VMEM((times,) + square, narrow),
            pltpu.VMEM(square, narrow),
            pltpu.VMEM(square, narrow),
            pltpu.VMEM(square, narrow),
            pltpu.VMEM((rows, states), narrow),
            pltpu.VMEM((rows, states), narrow),
            pltpu.VMEM((2 * rows, states), narrow),
            pltpu.VMEM(square, narrow),
            pltpu.VMEM(square, narrow),
            pltpu.VMEM(square, narrow),
            pltpu.VMEM(square, narrow),
            pltpu.VMEM(square, narrow),
            pltpu.VMEM((states + rows, states), wide),
            pltpu.VMEM((rows, states), wide),
            pltpu.VMEM((times, rows, states), narrow),
            pltpu.VMEM((times, SUBLANES, LANES), wide),
            dma((6,)),
            dma,
            dma,
            dma,
            dma((times // 2 + 1,)),
            dma,
            dma((times // 2 + 1,)),
            dma,
            dma((times, 3)),
            dma,
            dma,
            dma,
            dma,
        ],
        compiler_params=pltpu.CompilerParams(
            collective_id=0, has_side_effects=True, vmem_limit_bytes=VMEM_GRANT
        ),
    )(sector_sizes, hyb_particle, hyb_hole, propagator, rising_op, energies)


def per_device(propagator, rising_op, energies, hyb_particle, hyb_hole, sector_sizes):
    times = lax.axis_size("tm")
    states = propagator.shape[-1]
    fits = (
        propagator.shape[1] == 1
        and times == (CORE | ACROSS | ALONG) + 1
        and states % (times * ROW_TILE) == 0
        and states % (PIECES * ROW_TILE) == 0
        and states % LANES == 0
    )
    chosen = fused_device if fits else general_device
    return chosen(propagator, rising_op, energies, hyb_particle, hyb_hole, sector_sizes)


def solution(mesh):
    placed = (
        P("sector", "tm", None, None),
        P("sector", None, None),
        P("sector", None),
        P("tm"),
        P("tm"),
        P("sector"),
    )
    return jax.shard_map(
        per_device,
        mesh=mesh,
        in_specs=placed,
        out_specs=P("sector", "tm", None, None),
        check_vma=False,
    )
```

```python
import functools
import jax
import jax.numpy as jnp
from jax import lax
from jax.experimental import pallas as pl
from jax.experimental.pallas import tpu as pltpu
from jax.sharding import PartitionSpec as P


def shifted(block, axis, distance):
    devices = range(lax.axis_size(axis))
    route = [(i - distance, i) for i in devices if i - distance in devices]
    return lax.ppermute(block, axis, route)


def general_device(propagator, rising_op, energies, hyb_particle, hyb_hole, sector_sizes):
    t_dev = propagator.shape[1]
    states = propagator.shape[2]
    time_count = t_dev * lax.axis_size("tm")
    step_size = 1.0 / time_count
    positions = jnp.arange(states, dtype=jnp.int32)
    live_mask = positions < sector_sizes[0]
    square = live_mask[:, None] & live_mask[None, :]
    masked_prop = jnp.where(square[None], propagator[0], jnp.zeros((), jnp.bfloat16))
    operator = rising_op[0]
    raised = jnp.einsum(
        "ik,tkl->til", operator, masked_prop, preferred_element_type=jnp.float32
    ).astype(jnp.bfloat16)
    upward = jnp.einsum("tik,jk->tij", raised, operator, preferred_element_type=jnp.float32).astype(
        jnp.bfloat16
    )
    from_below = shifted(upward, "sector", 1)
    from_above = shifted(masked_prop, "sector", -1)
    lowered = jnp.einsum(
        "ki,tkl->til", operator, from_above, preferred_element_type=jnp.float32
    ).astype(jnp.bfloat16)
    downward = jnp.einsum("tik,kl->til", lowered, operator, preferred_element_type=jnp.float32)
    combined = (
        hyb_particle[:, None, None] * from_below.astype(jnp.float32)
        + hyb_hole[:, None, None] * downward
    )
    self_energy = jnp.where(square[None], combined, jnp.zeros((), jnp.float32)).astype(jnp.bfloat16)
    rows_each = states // lax.axis_size("tm")
    first_row = lax.axis_index("tm") * rows_each
    lag_rows = lax.all_to_all(self_energy, "tm", split_axis=1, concat_axis=0, tiled=True)
    history = lax.all_gather(masked_prop, "tm", axis=0, tiled=True)
    mirrored = jnp.concatenate([history[::-1], history], 0)
    slots = jnp.arange(time_count, dtype=jnp.int32)
    wide_slots = jnp.arange(time_count + 1, dtype=jnp.int32)

    def pair_step(lag, sums):
        forward, backward = sums
        other = time_count - 1 - lag
        window = lax.dynamic_slice_in_dim(mirrored, lag, time_count + 1, 0)
        near = lax.dynamic_index_in_dim(lag_rows, lag, 0, keepdims=False)
        far = lax.dynamic_index_in_dim(lag_rows, other, 0, keepdims=False)
        left = jnp.where((wide_slots < time_count - lag)[:, None, None], near[None], far[None])
        product = jnp.einsum("uik,ukl->uil", left, window, preferred_element_type=jnp.float32)
        backward = backward + jnp.where(
            (slots < time_count - lag)[:, None, None],
            product[:time_count],
            jnp.zeros((), jnp.float32),
        )
        forward = forward + jnp.where(
            (slots >= time_count - lag - 1)[:, None, None], product[1:], jnp.zeros((), jnp.float32)
        )
        return (forward, backward)

    empty_rows = jnp.zeros((time_count, rows_each, states), jnp.float32)
    forward, backward = lax.fori_loop(0, time_count // 2, pair_step, (empty_rows, empty_rows))
    convolved = step_size * (forward + backward[::-1])
    row_ids = first_row + jnp.arange(rows_each, dtype=jnp.int32)
    row_rates = lax.dynamic_slice_in_dim(energies[0], first_row, rows_each, 0)
    decay_rows = jnp.exp(-step_size * row_rates)

    def advance(running, term):
        running = decay_rows[:, None] * running + term
        return (running, running)

    _, summed = lax.scan(advance, jnp.zeros((rows_each, states), jnp.float32), convolved)
    moments = jnp.arange(time_count).astype(jnp.float32) * step_size
    live_rows = row_ids < sector_sizes[0]
    free_part = jnp.where(
        live_rows[None, :],
        jnp.exp(-row_rates[None, :] * moments[:, None]),
        jnp.zeros((), jnp.float32),
    )
    diagonal = jnp.where(
        (row_ids[:, None] == positions[None, :])[None],
        free_part[:, :, None],
        jnp.zeros((), jnp.float32),
    )
    new_rows = (diagonal - step_size * summed).astype(jnp.bfloat16)
    return lax.all_to_all(new_rows, "tm", split_axis=0, concat_axis=1, tiled=True)[None]


MESH = pl.DeviceIdType.MESH
ROW_TILE = 16
LANES = 128
SUBLANES = 8
CORE, ACROSS, ALONG = 1, 2, 4
PIECES = 4
VMEM_GRANT = 211 * 2**18


def flipped(index, mask):
    bit = 1
    while bit <= mask:
        if mask & bit:
            index = index + bit - 2 * bit * lax.rem(lax.div(index, bit), 2)
        bit *= 2
    return index


def fused_kernel(
    times,
    sectors,
    size_hbm,
    particle_hbm,
    hole_hbm,
    prop_hbm,
    operator_hbm,
    energy_hbm,
    out_ref,
    size_ref,
    particle_ref,
    hole_ref,
    energy_ref,
    history,
    operator,
    raiser,
    raiser_turned,
    turned,
    turned_in,
    pair,
    up_rows,
    down_rows,
    below,
    above,
    energy_in,
    sums,
    running,
    fresh,
    strengths,
    load_sem,
    turned_send,
    turned_recv,
    up_send,
    up_recv,
    down_send,
    down_recv,
    piece_send,
    piece_recv,
    strength_send,
    strength_recv,
    out_send,
    out_recv,
):
    states = prop_hbm.shape[-1]
    rows = states // times
    quarter = states // PIECES
    step_size = 1.0 / times
    me = lax.axis_index("tm")
    sector = lax.axis_index("sector")
    has_below = sector > 0
    has_above = sector < sectors - 1
    core = lax.rem(me, 2)
    even = me - core
    partner = flipped(me, CORE)
    x_even, y_even = flipped(even, ACROSS), flipped(even, ALONG)
    d_even = flipped(even, ACROSS | ALONG)

    loads = [
        pltpu.make_async_copy(src, dst, load_sem.at[i])
        for i, (src, dst) in enumerate(
            [
                (prop_hbm.at[0, 0], history.at[me]),
                (size_hbm, size_ref),
                (operator_hbm.at[0], operator),
                (particle_hbm, particle_ref),
                (hole_hbm, hole_ref),
                (energy_hbm, energy_ref),
            ]
        )
    ]
    barrier = pltpu.get_barrier_semaphore()
    for mask in range(1, times):
        pl.semaphore_signal(
            barrier, inc=1, device_id={"tm": flipped(me, mask)}, device_id_type=MESH
        )

    @pl.when(has_below)
    def _():
        pl.semaphore_signal(barrier, inc=1, device_id={"sector": sector - 1}, device_id_type=MESH)

    @pl.when(has_above)
    def _():
        pl.semaphore_signal(barrier, inc=1, device_id={"sector": sector + 1}, device_id_type=MESH)

    for load in loads:
        load.start()

    def row_block(index):
        return pl.ds(pl.multiple_of(index * rows, rows), rows)

    def piece_copy(step, time, q, kind):
        piece = history.at[time, pl.ds(pl.multiple_of(q * quarter, quarter), quarter)]
        return pltpu.make_async_remote_copy(
            src_ref=piece,
            dst_ref=piece,
            send_sem=piece_send,
            recv_sem=piece_recv.at[time, kind],
            device_id={"tm": flipped(me, step)},
            device_id_type=MESH,
        )

    mine = [2 * core, 2 * core + 1]
    other = [2 - 2 * core, 3 - 2 * core]

    def turned_copy(step=1):
        return pltpu.make_async_remote_copy(
            src_ref=turned,
            dst_ref=turned_in,
            send_sem=turned_send,
            recv_sem=turned_recv,
            device_id={"sector": sector + step},
            device_id_type=MESH,
        )

    def signal_of(slot):
        return slot // 2 if slot < times - 2 else slot - times // 2 + 1

    def up_copy(slot, time, step=1):
        block = row_block(time)
        return pltpu.make_async_remote_copy(
            src_ref=up_rows.at[block],
            dst_ref=below.at[block],
            send_sem=up_send,
            recv_sem=up_recv.at[signal_of(slot)],
            device_id={"sector": sector + step},
            device_id_type=MESH,
        )

    def down_copy(slot, time, step=-1):
        block = row_block(time)
        return pltpu.make_async_remote_copy(
            src_ref=down_rows.at[block],
            dst_ref=above.at[block],
            send_sem=down_send,
            recv_sem=down_recv.at[signal_of(slot)],
            device_id={"sector": sector + step},
            device_id_type=MESH,
        )

    def strength_copy(mask, block, count=1):
        return pltpu.make_async_remote_copy(
            src_ref=strengths.at[pl.ds(block, count)],
            dst_ref=strengths.at[pl.ds(block, count)],
            send_sem=strength_send,
            recv_sem=strength_recv,
            device_id={"tm": flipped(me, mask)},
            device_id_type=MESH,
        )

    def out_copy(moment, place):
        return pltpu.make_async_remote_copy(
            src_ref=fresh.at[moment],
            dst_ref=out_ref.at[0, 0, row_block(place)],
            send_sem=out_send,
            recv_sem=out_recv,
            device_id={"tm": moment},
            device_id_type=MESH,
        )

    loads[0].wait()
    for load in loads[3:]:
        load.wait()
    first_line = lax.broadcasted_iota(jnp.int32, strengths.shape[1:], 0) == 0
    strengths[me] = jnp.where(first_line, particle_ref[0], hole_ref[0])
    neighbours = jnp.where(has_below, 1, 0) + jnp.where(has_above, 1, 0)
    pl.semaphore_wait(barrier, times - 1 + neighbours)

    def links_start(time):
        for step, r in ((ACROSS, 0), (ALONG, 1), (ACROSS, 1), (ALONG, 0)):
            piece_copy(step, time, mine[r], r).start()

    def share_start(time):
        for q in mine:
            piece_copy(CORE, time, q, 2).start()

    for mask in range(1, times):
        strength_copy(mask, me).start()
    for r, q in enumerate(other):
        piece_copy(CORE, me, q, r).start()

    @pl.when(core == 0)
    def _():
        links_start(me)

    share_start(me)
    loads[2].wait()
    row_ids = me * rows + lax.broadcasted_iota(jnp.int32, (rows, states), 0)
    column_ids = lax.broadcasted_iota(jnp.int32, (rows, states), 1)
    on_diagonal = row_ids == column_ids
    chosen = jnp.where(on_diagonal, 1.0, 0.0).astype(jnp.bfloat16)
    turned[...] = lax.dot_general(
        chosen, operator[...], (((1,), (1,)), ((), ())), preferred_element_type=jnp.float32
    ).astype(jnp.bfloat16)

    @pl.when(has_above)
    def _():
        turned_copy().start()

    loads[1].wait()
    size = size_ref[0]
    live_columns = lax.broadcasted_iota(jnp.int32, (states, states), 1) < size
    live_line = column_ids < size
    raiser[...] = jnp.where(live_columns, operator[...].astype(jnp.float32), 0.0).astype(
        jnp.bfloat16
    )
    for r, q in enumerate(mine):
        piece_copy(CORE, partner, q, r).wait_recv()

    links_start(partner)

    @pl.when(core == 1)
    def _():
        links_start(me)

    def product_of(left, time):
        return jnp.dot(left, history[time], preferred_element_type=jnp.float32)

    def send_up(slot, time, raised):
        up_rows[row_block(time)] = jnp.dot(
            raised.astype(jnp.bfloat16), raiser_turned[...], preferred_element_type=jnp.float32
        ).astype(jnp.bfloat16)

        @pl.when(has_above)
        def _():
            up_copy(slot, time).start()

    def send_down(slot, time, lowered):
        down_rows[row_block(time)] = jnp.where(live_line, lowered, 0.0).astype(jnp.bfloat16)

        @pl.when(has_below)
        def _():
            down_copy(slot, time).start()

    def arrive(step, time, r):
        piece_copy(step, time, mine[r], r).wait_recv()
        piece_copy(CORE, time, mine[r], 2).start()

    def relay(step, time, r):
        piece_copy(step, time, mine[r], r).start()

    def shared(time):
        rest = history.at[time, pl.ds(0, states // 2)]
        pltpu.make_async_remote_copy(
            src_ref=rest,
            dst_ref=rest,
            send_sem=piece_send,
            recv_sem=piece_recv.at[time, 2],
            device_id={"tm": partner},
            device_id_type=MESH,
        ).wait_recv()

    order = [me, partner, x_even, y_even, x_even + 1, y_even + 1, d_even, d_even + 1]
    last = order[-1]

    pair[0:rows] = raiser[row_block(me)]
    raiser_turned[...] = raiser[...].T
    send_up(0, me, product_of(pair[0:rows], me))
    shared(partner)
    send_up(1, partner, product_of(pair[0:rows], partner))

    rates = jnp.sum(
        jnp.where(on_diagonal, energy_ref[...], jnp.zeros((), jnp.float32)), axis=1, keepdims=True
    )
    decay = jnp.exp(-step_size * rates)
    running[...] = jnp.zeros_like(running)
    sums[...] = jnp.zeros_like(sums)

    @pl.when(jnp.logical_not(has_below))
    def _():
        turned_in[...] = jnp.zeros_like(turned_in)
        below[...] = jnp.zeros_like(below)

    @pl.when(jnp.logical_not(has_above))
    def _():
        above[...] = jnp.zeros_like(above)

    arrive(ACROSS, x_even, 0)
    relay(ALONG, x_even, 0)
    arrive(ALONG, y_even, 1)
    relay(ACROSS, y_even, 1)

    @pl.when(has_below)
    def _():
        turned_copy(-1).wait_recv()

    pair[rows : 2 * rows] = jnp.where(
        live_line, turned_in[...].astype(jnp.float32), 0.0
    ).astype(jnp.bfloat16)
    for slot in range(2):
        send_down(slot, order[slot], product_of(pair[rows : 2 * rows], order[slot]))

    arrive(ACROSS, x_even, 1)
    arrive(ALONG, y_even, 0)

    def both(slot):
        time = order[slot]
        shared(time)
        result = product_of(pair[...], time)
        send_down(slot, time, result[rows : 2 * rows])
        send_up(slot, time, result[0:rows])

    live_rows = (row_ids < size) & (column_ids < size)
    shown = on_diagonal & (row_ids < size)

    def wait_rows(buffer, send, recv, slots, step):
        block = buffer.at[pl.ds(0, len(slots) * rows)]
        pltpu.make_async_remote_copy(
            src_ref=block,
            dst_ref=block,
            send_sem=send,
            recv_sem=recv.at[signal_of(slots[0])],
            device_id={"sector": sector + step},
            device_id_type=MESH,
        ).wait_recv()

    def combine(*slots):
        places = [row_block(order[slot]) for slot in slots]

        @pl.when(has_below)
        def _():
            wait_rows(below, up_send, up_recv, slots, -1)

        @pl.when(has_above)
        def _():
            wait_rows(above, down_send, down_recv, slots, 1)

        lowered = jnp.concatenate([above[place] for place in places], 0)
        downward = jnp.dot(lowered, operator[...], preferred_element_type=jnp.float32)
        for i, (slot, place) in enumerate(zip(slots, places)):
            level = strengths[order[slot]]
            combined = (
                level[0:1, 0:1] * below[place].astype(jnp.float32)
                + level[1:2, 0:1] * downward[i * rows : (i + 1) * rows]
            )
            energy_in[place] = jnp.where(live_rows, combined, jnp.zeros((), jnp.float32)).astype(
                jnp.bfloat16
            )

    def accumulate(lag_even, *bases):
        left = energy_in[pl.ds(pl.multiple_of(lag_even * rows, rows), 2 * rows)]
        for base in bases:
            first = pl.multiple_of((lag_even + base) * rows, rows)
            sums[pl.ds(first, 2 * rows)] += jnp.dot(
                left, history[base], preferred_element_type=jnp.float32
            )

    def convolve(lag_even, *bases):
        @pl.when(lag_even + bases[0] < times)
        def _():
            accumulate(lag_even, *bases)

    def finish(moment):
        place = row_block(moment)
        value = decay * running[...] + step_size * sums[place]
        running[...] = value
        instant = jnp.asarray(moment, jnp.int32).astype(jnp.float32) * step_size
        free_part = jnp.where(shown, jnp.exp(-rates * instant), jnp.zeros((), jnp.float32))
        fresh[moment] = jnp.where(
            live_rows, free_part - step_size * value, jnp.zeros((), jnp.float32)
        ).astype(jnp.bfloat16)

        @pl.when((me != moment))
        def _():
            out_copy(moment, me).start()

        @pl.when(me == moment)
        def _():
            out_ref[0, 0, row_block(me)] = fresh[moment]

    x_odd, y_odd = x_even + 1, y_even + 1
    strength_copy(CORE, 0, times - 1).wait_recv()
    both(2)
    both(3)
    combine(0, 1)
    convolve(even, even, even + 1)
    arrive(ACROSS, x_odd, 0)
    relay(ALONG, x_odd, 0)
    arrive(ALONG, y_odd, 1)
    relay(ACROSS, y_odd, 1)
    convolve(even, x_even)
    convolve(even, y_even)
    arrive(ACROSS, x_odd, 1)
    arrive(ALONG, y_odd, 0)
    combine(2, 3)
    both(4)
    both(5)
    arrive(ALONG, d_even, 0)
    arrive(ACROSS, d_even, 1)
    convolve(even, x_odd)
    convolve(even, y_odd)

    both(6)
    accumulate(even, d_even)

    @pl.when(even == 0)
    def _():
        sums[row_block(x_even)] += jnp.dot(
            energy_in[row_block(x_even)], history[0], preferred_element_type=jnp.float32
        )
        for moment in range(times // 4 + 1):
            finish(moment)

    arrive(ALONG, last, 0)
    arrive(ACROSS, last, 1)
    combine(4, 5)

    def finish_between(start, stop, allowed):
        for moment in range(start, stop, 2):

            @pl.when(allowed & (moment < d_even) & ((even != 0) | (moment > times // 4)))
            def _():
                finish(moment)

            @pl.when(allowed & (moment < d_even) & ((even != 0) | (moment + 1 > times // 4)))
            def _():
                finish(moment + 1)

    first_half = d_even >= times // 2

    def early(allowed):
        @pl.when(allowed)
        def _():
            convolve(x_even, even, even + 1)
            convolve(x_even, x_even, x_odd)
            finish_between(0, times // 2, first_half)
            convolve(y_even, y_even, y_odd)
            finish_between(0, times // 2, jnp.logical_not(first_half))

    early(even == 0)
    both(7)
    early(even != 0)
    convolve(x_even, d_even, last)
    convolve(y_even, d_even, last)

    def finish_next(allowed):
        @pl.when(allowed)
        def _():
            combine(6)
            sums[row_block(d_even)] += jnp.dot(
                energy_in[row_block(d_even)], history[0], preferred_element_type=jnp.float32
            )
            finish(d_even)

    finish_next(even != 0)
    accumulate(x_even, y_even, y_odd)
    accumulate(y_even, x_even, x_odd)
    convolve(y_even, even, even + 1)
    finish_between(times // 2, times, first_half)
    finish_next(even == 0)
    accumulate(even, last)
    combine(7)
    for moment in range(0, times, 2):

        @pl.when(d_even + moment < times)
        def _():
            accumulate(d_even, moment, moment + 1)
            if moment > 0:
                finish(d_even + moment)
            finish(d_even + moment + 1)

    strength_copy(CORE, 0, times - 1).wait_send()
    blocks = history.at[pl.ds(0, times - 1)]
    pltpu.make_async_remote_copy(
        src_ref=blocks,
        dst_ref=blocks,
        send_sem=piece_send,
        recv_sem=piece_recv.at[0, 0],
        device_id={"tm": partner},
        device_id_type=MESH,
    ).wait_send()

    def wait_sent(buffer, send, recv, step):
        pltpu.make_async_remote_copy(
            src_ref=buffer,
            dst_ref=buffer,
            send_sem=send,
            recv_sem=recv.at[0],
            device_id={"sector": sector + step},
            device_id_type=MESH,
        ).wait_send()

    @pl.when(has_below)
    def _():
        wait_sent(down_rows, down_send, down_recv, -1)

    @pl.when(has_above)
    def _():
        turned_copy().wait_send()
        wait_sent(up_rows, up_send, up_recv, 1)

    results = fresh.at[pl.ds(0, times - 1)]
    leaving = pltpu.make_async_remote_copy(
        src_ref=results,
        dst_ref=results,
        send_sem=out_send,
        recv_sem=out_recv,
        device_id={"tm": partner},
        device_id_type=MESH,
    )
    leaving.wait_recv()
    leaving.wait_send()


def fused_device(propagator, rising_op, energies, hyb_particle, hyb_hole, sector_sizes):
    times = lax.axis_size("tm")
    states = propagator.shape[-1]
    rows = states // times
    square = (states, states)
    narrow, wide = jnp.bfloat16, jnp.float32
    anywhere = pl.BlockSpec(memory_space=pltpu.HBM)
    dma = pltpu.SemaphoreType.DMA
    return pl.pallas_call(
        functools.partial(fused_kernel, times, lax.axis_size("sector")),
        out_shape=jax.ShapeDtypeStruct(propagator.shape, narrow),
        in_specs=[anywhere] * 6,
        out_specs=pl.BlockSpec(memory_space=pltpu.VMEM),
        scratch_shapes=[
            pltpu.SMEM((1,), jnp.int32),
            pltpu.SMEM((1,), wide),
            pltpu.SMEM((1,), wide),
            pltpu.VMEM(energies.shape, wide),
            pltpu.VMEM((times,) + square, narrow),
            pltpu.VMEM(square, narrow),
            pltpu.VMEM(square, narrow),
            pltpu.VMEM(square, narrow),
            pltpu.VMEM((rows, states), narrow),
            pltpu.VMEM((rows, states), narrow),
            pltpu.VMEM((2 * rows, states), narrow),
            pltpu.VMEM(square, narrow),
            pltpu.VMEM(square, narrow),
            pltpu.VMEM(square, narrow),
            pltpu.VMEM(square, narrow),
            pltpu.VMEM(square, narrow),
            pltpu.VMEM((states + rows, states), wide),
            pltpu.VMEM((rows, states), wide),
            pltpu.VMEM((times, rows, states), narrow),
            pltpu.VMEM((times, SUBLANES, LANES), wide),
            dma((6,)),
            dma,
            dma,
            dma,
            dma((times // 2 + 1,)),
            dma,
            dma((times // 2 + 1,)),
            dma,
            dma((times, 3)),
            dma,
            dma,
            dma,
            dma,
        ],
        compiler_params=pltpu.CompilerParams(
            collective_id=0, has_side_effects=True, vmem_limit_bytes=VMEM_GRANT
        ),
    )(sector_sizes, hyb_particle, hyb_hole, propagator, rising_op, energies)


def per_device(propagator, rising_op, energies, hyb_particle, hyb_hole, sector_sizes):
    times = lax.axis_size("tm")
    states = propagator.shape[-1]
    fits = (
        propagator.shape[1] == 1
        and times == (CORE | ACROSS | ALONG) + 1
        and states % (times * ROW_TILE) == 0
        and states % (PIECES * ROW_TILE) == 0
        and states % LANES == 0
    )
    chosen = fused_device if fits else general_device
    return chosen(propagator, rising_op, energies, hyb_particle, hyb_hole, sector_sizes)


def solution(mesh):
    placed = (
        P("sector", "tm", None, None),
        P("sector", None, None),
        P("sector", None),
        P("tm"),
        P("tm"),
        P("sector"),
    )
    return jax.shard_map(
        per_device,
        mesh=mesh,
        in_specs=placed,
        out_specs=P("sector", "tm", None, None),
        check_vma=False,
    )
```

```python
import functools
import jax
import jax.numpy as jnp
from jax import lax
from jax.experimental import pallas as pl
from jax.experimental.pallas import tpu as pltpu
from jax.sharding import PartitionSpec as P


def shifted(block, axis, distance):
    devices = range(lax.axis_size(axis))
    route = [(i - distance, i) for i in devices if i - distance in devices]
    return lax.ppermute(block, axis, route)


def general_device(propagator, rising_op, energies, hyb_particle, hyb_hole, sector_sizes):
    t_dev = propagator.shape[1]
    states = propagator.shape[2]
    time_count = t_dev * lax.axis_size("tm")
    step_size = 1.0 / time_count
    positions = jnp.arange(states, dtype=jnp.int32)
    live_mask = positions < sector_sizes[0]
    square = live_mask[:, None] & live_mask[None, :]
    masked_prop = jnp.where(square[None], propagator[0], jnp.zeros((), jnp.bfloat16))
    operator = rising_op[0]
    raised = jnp.einsum(
        "ik,tkl->til", operator, masked_prop, preferred_element_type=jnp.float32
    ).astype(jnp.bfloat16)
    upward = jnp.einsum("tik,jk->tij", raised, operator, preferred_element_type=jnp.float32).astype(
        jnp.bfloat16
    )
    from_below = shifted(upward, "sector", 1)
    from_above = shifted(masked_prop, "sector", -1)
    lowered = jnp.einsum(
        "ki,tkl->til", operator, from_above, preferred_element_type=jnp.float32
    ).astype(jnp.bfloat16)
    downward = jnp.einsum("tik,kl->til", lowered, operator, preferred_element_type=jnp.float32)
    combined = (
        hyb_particle[:, None, None] * from_below.astype(jnp.float32)
        + hyb_hole[:, None, None] * downward
    )
    self_energy = jnp.where(square[None], combined, jnp.zeros((), jnp.float32)).astype(jnp.bfloat16)
    rows_each = states // lax.axis_size("tm")
    first_row = lax.axis_index("tm") * rows_each
    lag_rows = lax.all_to_all(self_energy, "tm", split_axis=1, concat_axis=0, tiled=True)
    history = lax.all_gather(masked_prop, "tm", axis=0, tiled=True)
    mirrored = jnp.concatenate([history[::-1], history], 0)
    slots = jnp.arange(time_count, dtype=jnp.int32)
    wide_slots = jnp.arange(time_count + 1, dtype=jnp.int32)

    def pair_step(lag, sums):
        forward, backward = sums
        other = time_count - 1 - lag
        window = lax.dynamic_slice_in_dim(mirrored, lag, time_count + 1, 0)
        near = lax.dynamic_index_in_dim(lag_rows, lag, 0, keepdims=False)
        far = lax.dynamic_index_in_dim(lag_rows, other, 0, keepdims=False)
        left = jnp.where((wide_slots < time_count - lag)[:, None, None], near[None], far[None])
        product = jnp.einsum("uik,ukl->uil", left, window, preferred_element_type=jnp.float32)
        backward = backward + jnp.where(
            (slots < time_count - lag)[:, None, None],
            product[:time_count],
            jnp.zeros((), jnp.float32),
        )
        forward = forward + jnp.where(
            (slots >= time_count - lag - 1)[:, None, None], product[1:], jnp.zeros((), jnp.float32)
        )
        return (forward, backward)

    empty_rows = jnp.zeros((time_count, rows_each, states), jnp.float32)
    forward, backward = lax.fori_loop(0, time_count // 2, pair_step, (empty_rows, empty_rows))
    convolved = step_size * (forward + backward[::-1])
    row_ids = first_row + jnp.arange(rows_each, dtype=jnp.int32)
    row_rates = lax.dynamic_slice_in_dim(energies[0], first_row, rows_each, 0)
    decay_rows = jnp.exp(-step_size * row_rates)

    def advance(running, term):
        running = decay_rows[:, None] * running + term
        return (running, running)

    _, summed = lax.scan(advance, jnp.zeros((rows_each, states), jnp.float32), convolved)
    moments = jnp.arange(time_count).astype(jnp.float32) * step_size
    live_rows = row_ids < sector_sizes[0]
    free_part = jnp.where(
        live_rows[None, :],
        jnp.exp(-row_rates[None, :] * moments[:, None]),
        jnp.zeros((), jnp.float32),
    )
    diagonal = jnp.where(
        (row_ids[:, None] == positions[None, :])[None],
        free_part[:, :, None],
        jnp.zeros((), jnp.float32),
    )
    new_rows = (diagonal - step_size * summed).astype(jnp.bfloat16)
    return lax.all_to_all(new_rows, "tm", split_axis=0, concat_axis=1, tiled=True)[None]


MESH = pl.DeviceIdType.MESH
ROW_TILE = 16
LANES = 128
SUBLANES = 8
CORE, ACROSS, ALONG = 1, 2, 4
PIECES = 4
VMEM_GRANT = 211 * 2**18


def flipped(index, mask):
    bit = 1
    while bit <= mask:
        if mask & bit:
            index = index + bit - 2 * bit * lax.rem(lax.div(index, bit), 2)
        bit *= 2
    return index


def fused_kernel(
    times,
    sectors,
    size_hbm,
    particle_hbm,
    hole_hbm,
    prop_hbm,
    operator_hbm,
    energy_hbm,
    out_ref,
    size_ref,
    particle_ref,
    hole_ref,
    energy_ref,
    history,
    operator,
    raiser,
    raiser_turned,
    turned,
    turned_in,
    pair,
    up_rows,
    down_rows,
    below,
    above,
    energy_in,
    sums,
    running,
    fresh,
    strengths,
    load_sem,
    turned_send,
    turned_recv,
    up_send,
    up_recv,
    down_send,
    down_recv,
    piece_send,
    piece_recv,
    strength_send,
    strength_recv,
    out_send,
    out_recv,
):
    states = prop_hbm.shape[-1]
    rows = states // times
    quarter = states // PIECES
    step_size = 1.0 / times
    me = lax.axis_index("tm")
    sector = lax.axis_index("sector")
    has_below = sector > 0
    has_above = sector < sectors - 1
    core = lax.rem(me, 2)
    even = me - core
    partner = flipped(me, CORE)
    x_even, y_even = flipped(even, ACROSS), flipped(even, ALONG)
    d_even = flipped(even, ACROSS | ALONG)

    loads = [
        pltpu.make_async_copy(src, dst, load_sem.at[i])
        for i, (src, dst) in enumerate(
            [
                (prop_hbm.at[0, 0], history.at[me]),
                (size_hbm, size_ref),
                (operator_hbm.at[0], operator),
                (particle_hbm, particle_ref),
                (hole_hbm, hole_ref),
                (energy_hbm, energy_ref),
            ]
        )
    ]
    barrier = pltpu.get_barrier_semaphore()
    for mask in range(1, times):
        pl.semaphore_signal(
            barrier, inc=1, device_id={"tm": flipped(me, mask)}, device_id_type=MESH
        )

    @pl.when(has_below)
    def _():
        pl.semaphore_signal(barrier, inc=1, device_id={"sector": sector - 1}, device_id_type=MESH)

    @pl.when(has_above)
    def _():
        pl.semaphore_signal(barrier, inc=1, device_id={"sector": sector + 1}, device_id_type=MESH)

    for load in loads:
        load.start()

    def row_block(index):
        return pl.ds(pl.multiple_of(index * rows, rows), rows)

    def piece_copy(step, time, q, kind):
        piece = history.at[time, pl.ds(pl.multiple_of(q * quarter, quarter), quarter)]
        return pltpu.make_async_remote_copy(
            src_ref=piece,
            dst_ref=piece,
            send_sem=piece_send,
            recv_sem=piece_recv.at[time, kind],
            device_id={"tm": flipped(me, step)},
            device_id_type=MESH,
        )

    mine = [2 * core, 2 * core + 1]
    other = [2 - 2 * core, 3 - 2 * core]

    def turned_copy(step=1):
        return pltpu.make_async_remote_copy(
            src_ref=turned,
            dst_ref=turned_in,
            send_sem=turned_send,
            recv_sem=turned_recv,
            device_id={"sector": sector + step},
            device_id_type=MESH,
        )

    def signal_of(slot):
        return slot // 2 if slot < times - 2 else slot - times // 2 + 1

    def up_copy(slot, time, step=1):
        block = row_block(time)
        return pltpu.make_async_remote_copy(
            src_ref=up_rows.at[block],
            dst_ref=below.at[block],
            send_sem=up_send,
            recv_sem=up_recv.at[signal_of(slot)],
            device_id={"sector": sector + step},
            device_id_type=MESH,
        )

    def down_copy(slot, time, step=-1):
        block = row_block(time)
        return pltpu.make_async_remote_copy(
            src_ref=down_rows.at[block],
            dst_ref=above.at[block],
            send_sem=down_send,
            recv_sem=down_recv.at[signal_of(slot)],
            device_id={"sector": sector + step},
            device_id_type=MESH,
        )

    def strength_copy(mask, block, count=1):
        return pltpu.make_async_remote_copy(
            src_ref=strengths.at[pl.ds(block, count)],
            dst_ref=strengths.at[pl.ds(block, count)],
            send_sem=strength_send,
            recv_sem=strength_recv,
            device_id={"tm": flipped(me, mask)},
            device_id_type=MESH,
        )

    def out_copy(moment, place):
        return pltpu.make_async_remote_copy(
            src_ref=fresh.at[moment],
            dst_ref=out_ref.at[0, 0, row_block(place)],
            send_sem=out_send,
            recv_sem=out_recv,
            device_id={"tm": moment},
            device_id_type=MESH,
        )

    loads[0].wait()
    for load in loads[3:]:
        load.wait()
    first_line = lax.broadcasted_iota(jnp.int32, strengths.shape[1:], 0) == 0
    strengths[me] = jnp.where(first_line, particle_ref[0], hole_ref[0])
    neighbours = jnp.where(has_below, 1, 0) + jnp.where(has_above, 1, 0)
    pl.semaphore_wait(barrier, times - 1 + neighbours)

    def links_start(time):
        for step, r in ((ACROSS, 0), (ALONG, 1), (ACROSS, 1), (ALONG, 0)):
            piece_copy(step, time, mine[r], r).start()

    def share_start(time):
        for q in mine:
            piece_copy(CORE, time, q, 2).start()

    for mask in range(1, times):
        strength_copy(mask, me).start()
    for r, q in enumerate(other):
        piece_copy(CORE, me, q, r).start()

    @pl.when(core == 0)
    def _():
        links_start(me)

    share_start(me)
    piece_copy(CORE, partner, mine[0], 0).wait_recv()
    piece_copy(ACROSS, partner, mine[0], 0).start()
    piece_copy(CORE, partner, mine[1], 1).wait_recv()
    piece_copy(ALONG, partner, mine[1], 1).start()
    piece_copy(ACROSS, partner, mine[1], 1).start()
    piece_copy(ALONG, partner, mine[0], 0).start()

    @pl.when(core == 1)
    def _():
        links_start(me)

    loads[2].wait()
    row_ids = me * rows + lax.broadcasted_iota(jnp.int32, (rows, states), 0)
    column_ids = lax.broadcasted_iota(jnp.int32, (rows, states), 1)
    on_diagonal = row_ids == column_ids
    chosen = jnp.where(on_diagonal, 1.0, 0.0).astype(jnp.bfloat16)
    turned[...] = lax.dot_general(
        chosen, operator[...], (((1,), (1,)), ((), ())), preferred_element_type=jnp.float32
    ).astype(jnp.bfloat16)

    @pl.when(has_above)
    def _():
        turned_copy().start()

    loads[1].wait()
    size = size_ref[0]
    live_columns = lax.broadcasted_iota(jnp.int32, (states, states), 1) < size
    live_line = column_ids < size
    raiser[...] = jnp.where(live_columns, operator[...].astype(jnp.float32), 0.0).astype(
        jnp.bfloat16
    )
    def product_of(left, time):
        return jnp.dot(left, history[time], preferred_element_type=jnp.float32)

    def send_up(slot, time, raised):
        up_rows[row_block(time)] = jnp.dot(
            raised.astype(jnp.bfloat16), raiser_turned[...], preferred_element_type=jnp.float32
        ).astype(jnp.bfloat16)

        @pl.when(has_above)
        def _():
            up_copy(slot, time).start()

    def send_down(slot, time, lowered):
        down_rows[row_block(time)] = jnp.where(live_line, lowered, 0.0).astype(jnp.bfloat16)

        @pl.when(has_below)
        def _():
            down_copy(slot, time).start()

    def arrive(step, time, r):
        piece_copy(step, time, mine[r], r).wait_recv()
        piece_copy(CORE, time, mine[r], 2).start()

    def relay(step, time, r):
        piece_copy(step, time, mine[r], r).start()

    def shared(time):
        rest = history.at[time, pl.ds(0, states // 2)]
        pltpu.make_async_remote_copy(
            src_ref=rest,
            dst_ref=rest,
            send_sem=piece_send,
            recv_sem=piece_recv.at[time, 2],
            device_id={"tm": partner},
            device_id_type=MESH,
        ).wait_recv()

    order = [me, partner, x_even, y_even, x_even + 1, y_even + 1, d_even, d_even + 1]
    last = order[-1]

    pair[0:rows] = raiser[row_block(me)]
    raiser_turned[...] = raiser[...].T
    send_up(0, me, product_of(pair[0:rows], me))
    shared(partner)
    send_up(1, partner, product_of(pair[0:rows], partner))

    rates = jnp.sum(
        jnp.where(on_diagonal, energy_ref[...], jnp.zeros((), jnp.float32)), axis=1, keepdims=True
    )
    decay = jnp.exp(-step_size * rates)
    running[...] = jnp.zeros_like(running)
    sums[...] = jnp.zeros_like(sums)

    @pl.when(jnp.logical_not(has_below))
    def _():
        turned_in[...] = jnp.zeros_like(turned_in)
        below[...] = jnp.zeros_like(below)

    @pl.when(jnp.logical_not(has_above))
    def _():
        above[...] = jnp.zeros_like(above)

    arrive(ACROSS, x_even, 0)
    relay(ALONG, x_even, 0)
    arrive(ALONG, y_even, 1)
    relay(ACROSS, y_even, 1)

    @pl.when(has_below)
    def _():
        turned_copy(-1).wait_recv()

    pair[rows : 2 * rows] = jnp.where(
        live_line, turned_in[...].astype(jnp.float32), 0.0
    ).astype(jnp.bfloat16)
    for slot in range(2):
        send_down(slot, order[slot], product_of(pair[rows : 2 * rows], order[slot]))

    arrive(ACROSS, x_even, 1)
    arrive(ALONG, y_even, 0)

    def both(slot):
        time = order[slot]
        shared(time)
        result = product_of(pair[...], time)
        send_down(slot, time, result[rows : 2 * rows])
        send_up(slot, time, result[0:rows])

    live_rows = (row_ids < size) & (column_ids < size)
    shown = on_diagonal & (row_ids < size)

    def wait_rows(buffer, send, recv, slots, step):
        block = buffer.at[pl.ds(0, len(slots) * rows)]
        pltpu.make_async_remote_copy(
            src_ref=block,
            dst_ref=block,
            send_sem=send,
            recv_sem=recv.at[signal_of(slots[0])],
            device_id={"sector": sector + step},
            device_id_type=MESH,
        ).wait_recv()

    def combine(*slots):
        places = [row_block(order[slot]) for slot in slots]

        @pl.when(has_below)
        def _():
            wait_rows(below, up_send, up_recv, slots, -1)

        @pl.when(has_above)
        def _():
            wait_rows(above, down_send, down_recv, slots, 1)

        lowered = jnp.concatenate([above[place] for place in places], 0)
        downward = jnp.dot(lowered, operator[...], preferred_element_type=jnp.float32)
        for i, (slot, place) in enumerate(zip(slots, places)):
            level = strengths[order[slot]]
            combined = (
                level[0:1, 0:1] * below[place].astype(jnp.float32)
                + level[1:2, 0:1] * downward[i * rows : (i + 1) * rows]
            )
            energy_in[place] = jnp.where(live_rows, combined, jnp.zeros((), jnp.float32)).astype(
                jnp.bfloat16
            )

    def accumulate(lag_even, *bases):
        left = energy_in[pl.ds(pl.multiple_of(lag_even * rows, rows), 2 * rows)]
        for base in bases:
            first = pl.multiple_of((lag_even + base) * rows, rows)
            sums[pl.ds(first, 2 * rows)] += jnp.dot(
                left, history[base], preferred_element_type=jnp.float32
            )

    def convolve(lag_even, *bases):
        @pl.when(lag_even + bases[0] < times)
        def _():
            accumulate(lag_even, *bases)

    def finish(moment):
        place = row_block(moment)
        value = decay * running[...] + step_size * sums[place]
        running[...] = value
        instant = jnp.asarray(moment, jnp.int32).astype(jnp.float32) * step_size
        free_part = jnp.where(shown, jnp.exp(-rates * instant), jnp.zeros((), jnp.float32))
        fresh[moment] = jnp.where(
            live_rows, free_part - step_size * value, jnp.zeros((), jnp.float32)
        ).astype(jnp.bfloat16)

        @pl.when((me != moment))
        def _():
            out_copy(moment, me).start()

        @pl.when(me == moment)
        def _():
            out_ref[0, 0, row_block(me)] = fresh[moment]

    x_odd, y_odd = x_even + 1, y_even + 1
    strength_copy(CORE, 0, times - 1).wait_recv()
    both(2)
    both(3)
    combine(0, 1)
    convolve(even, even, even + 1)
    arrive(ACROSS, x_odd, 0)
    relay(ALONG, x_odd, 0)
    arrive(ALONG, y_odd, 1)
    relay(ACROSS, y_odd, 1)
    convolve(even, x_even)
    convolve(even, y_even)
    arrive(ACROSS, x_odd, 1)
    arrive(ALONG, y_odd, 0)
    combine(2, 3)
    both(4)
    both(5)
    arrive(ALONG, d_even, 0)
    arrive(ACROSS, d_even, 1)
    convolve(even, x_odd)
    convolve(even, y_odd)

    both(6)
    accumulate(even, d_even)

    @pl.when(even == 0)
    def _():
        sums[row_block(x_even)] += jnp.dot(
            energy_in[row_block(x_even)], history[0], preferred_element_type=jnp.float32
        )
        for moment in range(times // 4 + 1):
            finish(moment)

    arrive(ALONG, last, 0)
    arrive(ACROSS, last, 1)
    combine(4, 5)

    def finish_between(start, stop, allowed):
        for moment in range(start, stop, 2):

            @pl.when(allowed & (moment < d_even) & ((even != 0) | (moment > times // 4)))
            def _():
                finish(moment)

            @pl.when(allowed & (moment < d_even) & ((even != 0) | (moment + 1 > times // 4)))
            def _():
                finish(moment + 1)

    first_half = d_even >= times // 2

    def early(allowed):
        @pl.when(allowed)
        def _():
            convolve(x_even, even, even + 1)
            convolve(x_even, x_even, x_odd)
            finish_between(0, times // 2, first_half)
            convolve(y_even, y_even, y_odd)
            finish_between(0, times // 2, jnp.logical_not(first_half))

    early(even == 0)

    def opposite(allowed):
        @pl.when(allowed)
        def _():
            accumulate(x_even, y_even, y_odd)

    opposite(even != 0)
    both(7)
    early(even != 0)
    convolve(x_even, d_even, last)
    convolve(y_even, d_even, last)

    def finish_next(allowed):
        @pl.when(allowed)
        def _():
            combine(6)
            sums[row_block(d_even)] += jnp.dot(
                energy_in[row_block(d_even)], history[0], preferred_element_type=jnp.float32
            )
            finish(d_even)

    finish_next(even != 0)
    opposite(even == 0)
    accumulate(y_even, x_even, x_odd)
    convolve(y_even, even, even + 1)
    finish_between(times // 2, times, first_half)
    finish_next(even == 0)
    accumulate(even, last)
    combine(7)
    for moment in range(0, times, 2):

        @pl.when(d_even + moment < times)
        def _():
            accumulate(d_even, moment, moment + 1)
            if moment > 0:
                finish(d_even + moment)
            finish(d_even + moment + 1)

    strength_copy(CORE, 0, times - 1).wait_send()
    blocks = history.at[pl.ds(0, times - 1)]
    pltpu.make_async_remote_copy(
        src_ref=blocks,
        dst_ref=blocks,
        send_sem=piece_send,
        recv_sem=piece_recv.at[0, 0],
        device_id={"tm": partner},
        device_id_type=MESH,
    ).wait_send()

    def wait_sent(buffer, send, recv, step):
        pltpu.make_async_remote_copy(
            src_ref=buffer,
            dst_ref=buffer,
            send_sem=send,
            recv_sem=recv.at[0],
            device_id={"sector": sector + step},
            device_id_type=MESH,
        ).wait_send()

    @pl.when(has_below)
    def _():
        wait_sent(down_rows, down_send, down_recv, -1)

    @pl.when(has_above)
    def _():
        turned_copy().wait_send()
        wait_sent(up_rows, up_send, up_recv, 1)

    results = fresh.at[pl.ds(0, times - 1)]
    leaving = pltpu.make_async_remote_copy(
        src_ref=results,
        dst_ref=results,
        send_sem=out_send,
        recv_sem=out_recv,
        device_id={"tm": partner},
        device_id_type=MESH,
    )
    leaving.wait_recv()
    leaving.wait_send()


def fused_device(propagator, rising_op, energies, hyb_particle, hyb_hole, sector_sizes):
    times = lax.axis_size("tm")
    states = propagator.shape[-1]
    rows = states // times
    square = (states, states)
    narrow, wide = jnp.bfloat16, jnp.float32
    anywhere = pl.BlockSpec(memory_space=pltpu.HBM)
    dma = pltpu.SemaphoreType.DMA
    return pl.pallas_call(
        functools.partial(fused_kernel, times, lax.axis_size("sector")),
        out_shape=jax.ShapeDtypeStruct(propagator.shape, narrow),
        in_specs=[anywhere] * 6,
        out_specs=pl.BlockSpec(memory_space=pltpu.VMEM),
        scratch_shapes=[
            pltpu.SMEM((1,), jnp.int32),
            pltpu.SMEM((1,), wide),
            pltpu.SMEM((1,), wide),
            pltpu.VMEM(energies.shape, wide),
            pltpu.VMEM((times,) + square, narrow),
            pltpu.VMEM(square, narrow),
            pltpu.VMEM(square, narrow),
            pltpu.VMEM(square, narrow),
            pltpu.VMEM((rows, states), narrow),
            pltpu.VMEM((rows, states), narrow),
            pltpu.VMEM((2 * rows, states), narrow),
            pltpu.VMEM(square, narrow),
            pltpu.VMEM(square, narrow),
            pltpu.VMEM(square, narrow),
            pltpu.VMEM(square, narrow),
            pltpu.VMEM(square, narrow),
            pltpu.VMEM((states + rows, states), wide),
            pltpu.VMEM((rows, states), wide),
            pltpu.VMEM((times, rows, states), narrow),
            pltpu.VMEM((times, SUBLANES, LANES), wide),
            dma((6,)),
            dma,
            dma,
            dma,
            dma((times // 2 + 1,)),
            dma,
            dma((times // 2 + 1,)),
            dma,
            dma((times, 3)),
            dma,
            dma,
            dma,
            dma,
        ],
        compiler_params=pltpu.CompilerParams(
            collective_id=0, has_side_effects=True, vmem_limit_bytes=VMEM_GRANT
        ),
    )(sector_sizes, hyb_particle, hyb_hole, propagator, rising_op, energies)


def per_device(propagator, rising_op, energies, hyb_particle, hyb_hole, sector_sizes):
    times = lax.axis_size("tm")
    states = propagator.shape[-1]
    fits = (
        propagator.shape[1] == 1
        and times == (CORE | ACROSS | ALONG) + 1
        and states % (times * ROW_TILE) == 0
        and states % (PIECES * ROW_TILE) == 0
        and states % LANES == 0
    )
    chosen = fused_device if fits else general_device
    return chosen(propagator, rising_op, energies, hyb_particle, hyb_hole, sector_sizes)


def solution(mesh):
    placed = (
        P("sector", "tm", None, None),
        P("sector", None, None),
        P("sector", None),
        P("tm"),
        P("tm"),
        P("sector"),
    )
    return jax.shard_map(
        per_device,
        mesh=mesh,
        in_specs=placed,
        out_specs=P("sector", "tm", None, None),
        check_vma=False,
    )
```
